128 devices in a mesh: row: 8 (over z, x_hi), col: 16 (over x_lo, y, core).
Axes of the slice: x: 4 (x_hi: 2, x_lo: 2; x = x_hi * 2 + x_lo), y: 4, z: 4, core: 2. Of those that a mesh axis runs over, the one named last changes fastest.
Arguments:
- dens_real: float32 [8192, 8192], P('row', 'col'), as said below
- dens_imag: float32 [8192, 8192], P('row', 'col'), as said below
- upper_band: float32 [8192, 384], P('row'), may hold values from -0.3 to 0.3
- pattern: int32 [64, 2], P('row'), may hold values 0 or 1
Outputs:
- new_real: float32 [8192, 8192], P('row', 'col')
- new_imag: float32 [8192, 8192], P('row', 'col')
The draws below stay inside these ranges and needn't reach their ends.
Inputs may be any that keep to these rules, and one draw needn't show every extreme that they name: dens_real is symmetric. dens_imag is antisymmetric, with a zero diagonal.
All inputs are finite; a program needn't handle non-finite values. No bound on the sum of `pattern` on one device may be relied on, other than what follows from the above.
Results may differ from the reference program's by a relative error of at most 0.0001.
Values sent between devices are 32-bit elements; how exact they have to be, the bound alone decides.
A program may use at most 128 MiB of HBM per device.

```python
import jax
import jax.numpy as jnp
from jax import lax

N = 8192
BS = 128
KB = 2
NB = 64


def draw_dens_real(key, part):
    normal_draw = jax.random.normal(jax.random.fold_in(key, 11), (N, N), jnp.float32)
    symmetric = (normal_draw + normal_draw.T) * 0.7071
    return symmetric


def draw_dens_imag(key, part):
    normal_draw = jax.random.normal(jax.random.fold_in(key, 21), (N, N), jnp.float32)
    antisym = (normal_draw - normal_draw.T) * 0.7071
    return antisym


def place_ends(entries, stream_key, low, high):
    longest = entries.shape.index(max(entries.shape))
    spots = []
    for shift in (0, 1):
        where = [jax.random.randint(jax.random.fold_in(stream_key, axis), (), 0, length) for axis, length in enumerate(entries.shape)]
        where[longest] = (where[longest] + shift) % entries.shape[longest]
        spots.append(tuple(where))
    return entries.at[spots[0]].set(low).at[spots[1]].set(high)


def level_of(key, shape, shards, low, top_value):
    factor_of, own = 1.0, jax.random.fold_in(key, 6)
    for axis_at, parts in shards:
        steps = jnp.exp(jax.random.uniform(jax.random.fold_in(own, axis_at), (parts,), jnp.float32, low / len(shards), top_value / len(shards)))
        factor_of = factor_of * jnp.repeat(steps, shape[axis_at] // parts).reshape([-1 if axis == axis_at else 1 for axis in range(len(shape))])
    return factor_of


def scatter_about(key, dims, deviation, reach, shards=(), held_as=jnp.bfloat16):
    array = jax.random.normal(key, dims, jnp.float32) * deviation
    if len(shards) > 0:
        array = level_of(key, dims, shards, -0.22, 0.18) * array
    return jnp.clip(array, min=-reach, max=reach).astype(held_as)


def setup_inputs(seed: int = 0) -> dict:
    keys = jax.random.split(jax.random.key(seed), 5)
    return {
        "dens_real": draw_dens_real(jax.random.fold_in(keys[4], 71), 0),
        "dens_imag": draw_dens_imag(jax.random.fold_in(keys[4], 71), 0),
        "upper_band": scatter_about(keys[2], (N, (KB + 1) * BS), 0.05, 0.3, ((0, 8),), jnp.float32),
        "pattern": place_ends((jax.random.randint(keys[3], (NB, KB), 0, 5) < 3).astype(jnp.int32), jax.random.fold_in(keys[3], 1), 0, 1),
    }


HIGHEST_PRECISION = lax.Precision.HIGHEST
STEP_TIME = 0.3


def masked_band(upper_band, pattern, first_block):
    block_count = pattern.shape[0]
    blocks = upper_band.reshape(block_count, BS, KB + 1, BS)
    block_index = first_block + jnp.arange(block_count, dtype=jnp.int32)
    offsets = jnp.arange(1, KB + 1, dtype=jnp.int32)
    present = (pattern > 0) & (block_index[:, None] + offsets[None, :] < NB)
    factor = jnp.concatenate([jnp.ones((block_count, 1), jnp.float32), present.astype(jnp.float32)], axis=1)
    return (blocks * factor[:, None, :, None]).reshape(block_count * BS, (KB + 1) * BS)


def build_tiles(masked_ext, block_count):
    blocks = masked_ext.reshape(block_count + KB, BS, KB + 1, BS)
    tile_list = []
    for k in range(2 * KB + 1):
        offset_block = k - KB
        if offset_block < 0:
            distance = -offset_block
            piece_rows = blocks[KB - distance:KB - distance + block_count, :, distance, :]
            tile_list.append(jnp.swapaxes(piece_rows, 1, 2))
        elif offset_block == 0:
            piece_rows = blocks[KB:, :, 0, :]
            tile_list.append(0.5 * (piece_rows + jnp.swapaxes(piece_rows, 1, 2)))
        else:
            tile_list.append(blocks[KB:, :, offset_block, :])
    return jnp.stack(tile_list, axis=2)


def row_product(tile_set, rows_ext):
    block_count = tile_set.shape[0]
    stacked = rows_ext.reshape(block_count + 2 * KB, BS, rows_ext.shape[1])
    summed = jnp.einsum("jab,jbn->jan", tile_set[:, :, 0, :], stacked[0:block_count], precision=HIGHEST_PRECISION)
    for k in range(1, 2 * KB + 1):
        summed = summed + jnp.einsum("jab,jbn->jan", tile_set[:, :, k, :], stacked[k:k + block_count], precision=HIGHEST_PRECISION)
    return summed.reshape(block_count * BS, rows_ext.shape[1])


def column_product(tile_set, columns_ext):
    block_count = tile_set.shape[0]
    row_total = columns_ext.shape[0]
    stacked = columns_ext.reshape(row_total, block_count + 2 * KB, BS)
    summed = jnp.einsum("njb,jcb->njc", stacked[:, 0:block_count], tile_set[:, :, 0, :], precision=HIGHEST_PRECISION)
    for k in range(1, 2 * KB + 1):
        summed = summed + jnp.einsum("njb,jcb->njc", stacked[:, k:k + block_count], tile_set[:, :, k, :], precision=HIGHEST_PRECISION)
    return summed.reshape(row_total, block_count * BS)


def derivative(real_part, imag_part, tile_set):
    rim_width = KB * BS
    real_rows = jnp.pad(real_part, ((rim_width, rim_width), (0, 0)))
    imag_rows = jnp.pad(imag_part, ((rim_width, rim_width), (0, 0)))
    real_columns = jnp.pad(real_part, ((0, 0), (rim_width, rim_width)))
    imag_columns = jnp.pad(imag_part, ((0, 0), (rim_width, rim_width)))
    h_real = row_product(tile_set, real_rows)
    h_imag = row_product(tile_set, imag_rows)
    real_h = column_product(tile_set, real_columns)
    imag_h = column_product(tile_set, imag_columns)
    return h_imag - imag_h, real_h - h_real


def reference(dens_real, dens_imag, upper_band, pattern):
    masked = masked_band(upper_band, pattern, 0)
    masked_ext = jnp.pad(masked, ((KB * BS, 0), (0, 0)))
    tile_set = build_tiles(masked_ext, NB)
    first_real, first_imag = derivative(dens_real, dens_imag, tile_set)
    section_real = dens_real + STEP_TIME * first_real
    section_imag = dens_imag + STEP_TIME * first_imag
    second_real, second_imag = derivative(section_real, section_imag, tile_set)
    new_real = dens_real + 0.5 * STEP_TIME * (first_real + second_real)
    new_imag = dens_imag + 0.5 * STEP_TIME * (first_imag + second_imag)
    return new_real, new_imag
```

```python
import jax
import jax.numpy as jnp
from jax import lax
from jax.experimental import pallas as pl
from jax.experimental.pallas import tpu as pltpu
from jax.sharding import PartitionSpec as P

BS = 128
KB = 2
NB = 64
STEP_TIME = 0.3
MESH = pl.DeviceIdType.MESH
F32 = jnp.float32
BF16 = jnp.bfloat16
TR = 1024
TC = 512
W = KB * BS
NG = TR // W
NJ = TC // W
ROWS = 8
COLS = 16
PIECES = [(0, BS, 2 * BS, BS), (BS, BS, BS, 2 * BS)] + [(q * BS, BS, 0, 3 * BS) for q in range(2, 6)]
LATE = (0, 1)
EARLY = (2, 3, 4, 5)


def mult(x, n=W):
    return pl.multiple_of(x, n)


def split(x):
    hi = x.astype(BF16)
    return hi, (x - hi.astype(F32)).astype(BF16)


def kernel(a_ref, b_ref, m_ref, oa_ref, ob_ref, dens, grad, xs, rowbuf, colbuf, ext, band, hrow, ncol,
           lsem, osem, rs_s, rs_r, cs_s, cs_r, ab_s, ab_r, up_s, dn_s, cr_s, bd_r):
    r, c = lax.axis_index("row"), lax.axis_index("col")
    even, core = r % 2 == 0, c % 2
    k = c // 2
    z, zk = r // 2, k // 2
    dz = (z - zk + 4) % 4
    is_src = r == k
    other = (c + 8) % 16
    crosses = r == other // 2
    fwd_up = dz < 2
    fwd_dn = dz == 0
    a_row = jnp.where(even, r + 1, r - 1)
    b_row = jnp.where(even, r - 1, r + 1)
    has_b = (b_row >= 0) & (b_row < ROWS)
    cc_col = jnp.where(core == 0, c + 1, c - 1)
    cy_col = jnp.where(core == 0, c - 1, c + 1)
    has_y = (cy_col >= 0) & (cy_col < COLS)
    z_up, z_dn = (r + 2) % ROWS, (r + 6) % ROWS
    cross_row = jnp.where(even, r + 1, r - 1)
    first = r > 0
    last = r < ROWS - 1

    row_dev = ((a_row, c), (b_row, c))
    row_src = (mult(jnp.where(even, TR - W, 0)), mult(jnp.where(even, 0, TR - W)))
    row_dst = (mult(jnp.where(even, TR + W, 0)), mult(jnp.where(even, 0, TR + W)))
    col_dev = ((r, cc_col), (r, cy_col))
    col_src = (mult(jnp.where(core == 0, TC - W, 0)), mult(jnp.where(core == 0, 0, TC - W)))
    col_dst = (mult(jnp.where(core == 0, TC + W, 0)), mult(jnp.where(core == 0, 0, TC + W)))
    g_a = jnp.where(even, NG - 1, 0)
    ext_off = mult(core * TC, BS)

    def order(t):
        return jnp.where(t < 2, t + 1, jnp.where(t == 2, g_a, NG - 1 - g_a))

    def remote(src, dst, ss, rs, dev):
        return pltpu.make_async_remote_copy(src, dst, ss, rs, device_id=dev, device_id_type=MESH)

    def row_copy(s, slot, n):
        src = (a_ref, b_ref)[n] if s == 0 else grad.at[n]
        return remote(src.at[pl.ds(row_src[slot], W), :], rowbuf.at[s, slot, n], rs_s.at[s, slot, n], rs_r.at[s, slot, n], row_dev[slot])

    def col_copy(s, slot, n, g):
        src = (a_ref, b_ref)[n] if s == 0 else grad.at[n]
        rows = pl.ds(mult(g * W), W)
        return remote(src.at[rows, pl.ds(col_src[slot], W)], colbuf.at[s, slot, n, rows, :], cs_s.at[s, slot, n, g], cs_r.at[s, slot, n, g], col_dev[slot])

    def above_copy(q):
        r0, nr, c0, nc = PIECES[q]
        return remote(m_ref.at[TR - W + r0 : TR - W + r0 + nr, c0 : c0 + nc], ext.at[r0 : r0 + nr, c0 : c0 + nc], ab_s.at[q], ab_r.at[q], (jnp.minimum(r + 1, ROWS - 1), c))

    def piece(ref, q, off=None):
        r0, nr, c0, nc = PIECES[q]
        rows = pl.ds(r0, nr) if off is None else pl.ds(mult(off + r0, BS), nr)
        return ref.at[rows, pl.ds(c0, nc)]

    def up_copy(q):
        return remote(piece(band, q), piece(band, q), up_s.at[q], bd_r.at[q], (z_up, c))

    def dn_copy(q):
        return remote(piece(band, q), piece(band, q), dn_s.at[q], bd_r.at[q], (z_dn, c))

    def cross_copy(q):
        src = piece(ext, q, ext_off) if q in LATE else piece(m_ref, q, ext_off - W)
        return remote(src, piece(band, q), cr_s.at[q], bd_r.at[q], (cross_row, other))

    def forward(q):
        @pl.when(fwd_up)
        def _():
            up_copy(q).start()

        @pl.when(fwd_dn)
        def _():
            dn_copy(q).start()

    def own_piece(q):
        src = piece(ext, q, ext_off) if q in LATE else piece(m_ref, q, ext_off - W)
        return pltpu.make_async_copy(src, piece(band, q), lsem.at[3 + q])

    barrier = pltpu.get_barrier_semaphore()

    def greet(dev):
        pl.semaphore_signal(barrier, inc=1, device_id=dev, device_id_type=MESH)

    for dev in (row_dev[0], col_dev[0], (z_up, c), (z_dn, c), (cross_row, other)):
        greet(dev)

    @pl.when(has_b)
    def _():
        greet(row_dev[1])

    @pl.when(has_y)
    def _():
        greet(col_dev[1])

    loads = [
        pltpu.make_async_copy(a_ref, dens.at[0], lsem.at[0]),
        pltpu.make_async_copy(b_ref, dens.at[1], lsem.at[1]),
        pltpu.make_async_copy(m_ref, ext.at[W:, :], lsem.at[2]),
    ]

    @pl.when(is_src)
    def _():
        for q in EARLY:
            own_piece(q).start()

    for cp in loads:
        cp.start()

    @pl.when(jnp.logical_not(first))
    def _():
        ext[0:W, :] = jnp.zeros((W, 3 * BS), F32)

    pl.semaphore_wait(barrier, 5 + has_b.astype(jnp.int32) + has_y.astype(jnp.int32))

    @pl.when(last)
    def _():
        for q in LATE:
            above_copy(q).start()

    @pl.when(crosses)
    def _():
        for q in EARLY:
            cross_copy(q).start()

    for n in range(2):
        row_copy(0, 0, n).start()

    def start_cols(s, g):
        for n in range(2):
            col_copy(s, 0, n, g).start()

        @pl.when(has_y)
        def _():
            for n in range(2):
                col_copy(s, 1, n, g).start()

    @pl.loop(0, NG)
    def _(t):
        start_cols(0, order(t))

    @pl.when(has_b)
    def _():
        for n in range(2):
            row_copy(0, 1, n).start()

    @pl.when(is_src)
    def _():
        for q in EARLY:
            own_piece(q).wait()
            forward(q)

    @pl.when(jnp.logical_not(has_b))
    def _():
        for s in range(2):
            for n in range(2):
                for p in range(2):
                    xs[s, n, p, pl.ds(row_dst[1], W), :] = jnp.zeros((W, TC + 2 * W), BF16)

    @pl.when(jnp.logical_not(has_y))
    def _():
        for s in range(2):
            for n in range(2):
                for p in range(2):
                    xs[s, n, p, :, pl.ds(col_dst[1], W)] = jnp.zeros((TR + 2 * W, W), BF16)

    loads[0].wait()
    loads[1].wait()

    @pl.loop(0, 2 * NG)
    def _(i):
        n, g = i // NG, i % NG
        hi, lo = split(dens[n, pl.ds(mult(g * W), W), :])
        xs[0, n, 0, pl.ds(mult(W + g * W), W), W : W + TC] = hi
        xs[0, n, 1, pl.ds(mult(W + g * W), W), W : W + TC] = lo

    @pl.when(jnp.logical_not(is_src))
    def _():
        for q in EARLY:
            up_copy(q).wait_recv()
            forward(q)

    loads[2].wait()

    @pl.when(first)
    def _():
        for q in LATE:
            above_copy(q).wait_recv()

    @pl.when(crosses)
    def _():
        for q in LATE:
            cross_copy(q).start()

    @pl.when(is_src)
    def _():
        for q in LATE:
            own_piece(q).start()
        for q in LATE:
            own_piece(q).wait()
            forward(q)

    @pl.loop(0, TR // BS)
    def _(i):
        g, h = i // 2, i % 2
        rows = pl.ds(mult(h * BS, BS), BS)

        def put(pos, value):
            hi, lo = split(value * STEP_TIME)
            cols = pl.ds(mult(pos * BS, BS), BS)
            hrow[0, g, rows, cols] = hi
            hrow[1, g, rows, cols] = lo

        for d in range(-KB, KB + 1):
            u = ext[pl.ds(mult((i + KB + min(d, 0)) * BS, BS), BS), abs(d) * BS : (abs(d) + 1) * BS]
            value = u if d > 0 else u.T if d < 0 else 0.5 * (u + u.T)
            put(h + d + KB, value)
        put((1 - h) * (2 * KB + 1), jnp.zeros((BS, BS), F32))

    @pl.when(jnp.logical_not(is_src))
    def _():
        for q in LATE:
            up_copy(q).wait_recv()
            forward(q)

    @pl.loop(0, TC // BS)
    def _(i):
        j, h = i // 2, i % 2
        cols = pl.ds(mult(h * BS, BS), BS)

        def put(pos, value):
            hi, lo = split(value * -STEP_TIME)
            rows = pl.ds(mult(pos * BS, BS), BS)
            ncol[0, j, rows, cols] = hi
            ncol[1, j, rows, cols] = lo

        for d in range(-KB, KB + 1):
            u = band[pl.ds(mult((i + KB + min(d, 0)) * BS, BS), BS), abs(d) * BS : (abs(d) + 1) * BS]
            value = u if d < 0 else u.T if d > 0 else 0.5 * (u + u.T)
            put(h + d + KB, value)
        put((1 - h) * (2 * KB + 1), jnp.zeros((BS, BS), F32))

    def take_cols(s, slot, g):
        rows = pl.ds(mult(g * W), W)
        for n in range(2):
            col_copy(s, slot, n, g).wait_recv()
        for n in range(2):
            hi, lo = split(colbuf[s, slot, n, rows, :])
            xs[s, n, 0, pl.ds(mult(W + g * W), W), pl.ds(col_dst[slot], W)] = hi
            xs[s, n, 1, pl.ds(mult(W + g * W), W), pl.ds(col_dst[slot], W)] = lo

    def take_rows(s, slot):
        for n in range(2):
            row_copy(s, slot, n).wait_recv()
        for n in range(2):
            hi, lo = split(rowbuf[s, slot, n])
            xs[s, n, 0, pl.ds(row_dst[slot], W), W : W + TC] = hi
            xs[s, n, 1, pl.ds(row_dst[slot], W), W : W + TC] = lo

    def product(s, n, g, j):
        r0, c0 = mult(g * W), mult(j * W)
        hi, lo = xs.at[s, 1 - n, 0], xs.at[s, 1 - n, 1]
        row_h = hi[pl.ds(r0, 3 * W), pl.ds(mult(c0 + W), W)]
        row_l = lo[pl.ds(r0, 3 * W), pl.ds(mult(c0 + W), W)]
        col_h = hi[pl.ds(mult(r0 + W), W), pl.ds(c0, 3 * W)]
        col_l = lo[pl.ds(mult(r0 + W), W), pl.ds(c0, 3 * W)]
        h_h, h_l = hrow[0, g], hrow[1, g]
        n_h, n_l = ncol[0, j], ncol[1, j]
        lhs = jnp.concatenate([h_h, h_h, h_l, col_h, col_l, col_h], axis=1)
        rhs = jnp.concatenate([row_h, row_l, row_h, n_h, n_h, n_l], axis=0)
        total = jnp.dot(lhs, rhs, preferred_element_type=F32)
        return jnp.where(n == 0, 1.0, -1.0).astype(F32) * total

    def out_copy(n, g):
        rows = pl.ds(mult(g * W), W)
        return pltpu.make_async_copy(dens.at[n, rows, :], (oa_ref, ob_ref)[n].at[rows, :], osem.at[n, g])

    for s in range(2):

        @pl.loop(0, NG)
        def _(t):
            g = order(t)
            take_cols(s, 0, g)

            @pl.when(has_y)
            def _():
                take_cols(s, 1, g)

            @pl.when(t == 2)
            def _():
                take_rows(s, 0)

            @pl.when((t == 3) & has_b)
            def _():
                take_rows(s, 1)

            @pl.loop(0, 2 * NJ)
            def _(i):
                n, j = i // NJ, i % NJ
                value = product(s, n, g, j)
                rows, cols = pl.ds(mult(g * W), W), pl.ds(mult(j * W), W)
                if s == 0:
                    grad[n, rows, cols] = value
                    hi, lo = split(value)
                    xs[1, n, 0, pl.ds(mult(W + g * W), W), pl.ds(mult(W + j * W), W)] = hi
                    xs[1, n, 1, pl.ds(mult(W + g * W), W), pl.ds(mult(W + j * W), W)] = lo
                else:
                    dens[n, rows, cols] = dens[n, rows, cols] + grad[n, rows, cols] + 0.5 * value

            if s == 0:

                @pl.when(t == 2)
                def _():
                    for n in range(2):
                        row_copy(1, 0, n).start()

                @pl.when((t == 3) & has_b)
                def _():
                    for n in range(2):
                        row_copy(1, 1, n).start()

                start_cols(1, g)
            else:
                for n in range(2):
                    out_copy(n, g).start()

    for s in range(2):
        for n in range(2):
            row_copy(s, 0, n).wait_send()

        @pl.when(has_b)
        def _():
            for n in range(2):
                row_copy(s, 1, n).wait_send()

        @pl.loop(0, NG)
        def _(g):
            for n in range(2):
                col_copy(s, 0, n, g).wait_send()

            @pl.when(has_y)
            def _():
                for n in range(2):
                    col_copy(s, 1, n, g).wait_send()

    @pl.when(last)
    def _():
        for q in LATE:
            above_copy(q).wait_send()

    @pl.when(crosses)
    def _():
        for q in range(6):
            cross_copy(q).wait_send()

    @pl.when(fwd_up)
    def _():
        for q in range(6):
            up_copy(q).wait_send()

    @pl.when(fwd_dn)
    def _():
        for q in range(6):
            dn_copy(q).wait_send()

    @pl.loop(0, NG)
    def _(g):
        for n in range(2):
            out_copy(n, g).wait()


def masked_band(upper_band, pattern, first_block):
    block_count = pattern.shape[0]
    blocks = upper_band.reshape(block_count, BS, KB + 1, BS)
    block_index = first_block + jnp.arange(block_count, dtype=jnp.int32)
    offsets = jnp.arange(1, KB + 1, dtype=jnp.int32)
    present = (pattern > 0) & (block_index[:, None] + offsets[None, :] < NB)
    present = jnp.concatenate([jnp.ones((block_count, 1), bool), present], axis=1)
    lanes = jnp.repeat(present, BS, axis=1)
    rows = jnp.repeat(lanes, BS, axis=0)
    return jnp.where(rows, upper_band, 0.0)


def shards(dens_real, dens_imag, upper_band, pattern):
    first_block = lax.axis_index("row") * (TR // BS)
    masked = masked_band(upper_band, pattern, first_block)
    dma = pltpu.SemaphoreType.DMA
    anywhere = pl.BlockSpec(memory_space=pl.ANY)
    return pl.pallas_call(
        kernel,
        out_shape=(jax.ShapeDtypeStruct((TR, TC), F32),) * 2,
        in_specs=[anywhere] * 3,
        out_specs=(anywhere,) * 2,
        scratch_shapes=[
            pltpu.VMEM((2, TR, TC), F32),
            pltpu.VMEM((2, TR, TC), F32),
            pltpu.VMEM((2, 2, 2, TR + 2 * W, TC + 2 * W), BF16),
            pltpu.VMEM((2, 2, 2, W, TC), F32),
            pltpu.VMEM((2, 2, 2, TR, W), F32),
            pltpu.VMEM((TR + W, 3 * BS), F32),
            pltpu.VMEM((TC + W, 3 * BS), F32),
            pltpu.VMEM((2, NG, W, 3 * W), BF16),
            pltpu.VMEM((2, NJ, 3 * W, W), BF16),
            dma((9,)),
            dma((2, NG)),
            dma((2, 2, 2)),
            dma((2, 2, 2)),
            dma((2, 2, 2, NG)),
            dma((2, 2, 2, NG)),
            dma((2,)),
            dma((2,)),
            dma((6,)),
            dma((6,)),
            dma((6,)),
            dma((6,)),
        ],
        compiler_params=pltpu.CompilerParams(collective_id=0, has_side_effects=True, vmem_limit_bytes=63 << 20),
        name="heun",
    )(dens_real, dens_imag, masked)


def solution(mesh):
    in_specs = (P("row", "col"), P("row", "col"), P("row", None), P("row", None))
    out_specs = (P("row", "col"), P("row", "col"))
    return jax.shard_map(shards, mesh=mesh, in_specs=in_specs, out_specs=out_specs, check_vma=False)
```

```python
import jax
import jax.numpy as jnp
from jax import lax
from jax.experimental import pallas as pl
from jax.experimental.pallas import tpu as pltpu
from jax.sharding import PartitionSpec as P

BS = 128
KB = 2
NB = 64
STEP_TIME = 0.3
MESH = pl.DeviceIdType.MESH
F32 = jnp.float32
BF16 = jnp.bfloat16
TR = 1024
TC = 512
W = KB * BS
NG = TR // W
NJ = TC // W
ROWS = 8
COLS = 16
PIECES = [(0, BS, 2 * BS, BS), (BS, BS, BS, 2 * BS)] + [(q * BS, BS, 0, 3 * BS) for q in range(2, 6)]
LATE = (0, 1)
EARLY = (2, 3, 4, 5)


def mult(x, n=W):
    return pl.multiple_of(x, n)


def split(x):
    hi = x.astype(BF16)
    return hi, (x - hi.astype(F32)).astype(BF16)


def kernel(a_ref, b_ref, m_ref, oa_ref, ob_ref, dens, grad, xs, rowbuf, colbuf, ext, band, hrow, ncol,
           lsem, osem, rs_s, rs_r, cs_s, cs_r, ab_s, ab_r, up_s, dn_s, cr_s, bd_r):
    r, c = lax.axis_index("row"), lax.axis_index("col")
    even, core = r % 2 == 0, c % 2
    k = c // 2
    z, zk, half = r // 2, k // 2, r % 2
    dz = (z - zk + 4) % 4
    is_src = r == k
    near = half == k % 2
    a_row = jnp.where(even, r + 1, r - 1)
    b_row = jnp.where(even, r - 1, r + 1)
    has_b = (b_row >= 0) & (b_row < ROWS)
    cc_col = jnp.where(core == 0, c + 1, c - 1)
    cy_col = jnp.where(core == 0, c - 1, c + 1)
    has_y = (cy_col >= 0) & (cy_col < COLS)
    z_up, z_dn = (r + 2) % ROWS, (r + 6) % ROWS
    first = r > 0
    last = r < ROWS - 1

    row_dev = ((a_row, c), (b_row, c))
    row_src = (mult(jnp.where(even, TR - W, 0)), mult(jnp.where(even, 0, TR - W)))
    row_dst = (mult(jnp.where(even, TR + W, 0)), mult(jnp.where(even, 0, TR + W)))
    col_dev = ((r, cc_col), (r, cy_col))
    col_src = (mult(jnp.where(core == 0, TC - W, 0)), mult(jnp.where(core == 0, 0, TC - W)))
    col_dst = (mult(jnp.where(core == 0, TC + W, 0)), mult(jnp.where(core == 0, 0, TC + W)))
    g_a = jnp.where(even, NG - 1, 0)
    ext_off = mult(core * TC, BS)

    def order(s, t):
        if s == 0:
            return jnp.where(t == 0, g_a, jnp.where(t == 3, NG - 1 - g_a, t))
        return jnp.where(t < 2, t + 1, jnp.where(t == 2, g_a, NG - 1 - g_a))

    def remote(src, dst, ss, rs, dev):
        return pltpu.make_async_remote_copy(src, dst, ss, rs, device_id=dev, device_id_type=MESH)

    def row_copy(s, slot, n):
        src = (a_ref, b_ref)[n] if s == 0 else grad.at[n]
        return remote(src.at[pl.ds(row_src[slot], W), :], rowbuf.at[s, slot, n], rs_s.at[s, slot, n], rs_r.at[s, slot, n], row_dev[slot])

    def col_copy(s, slot, n, g):
        src = (a_ref, b_ref)[n] if s == 0 else grad.at[n]
        rows = pl.ds(mult(g * W), W)
        return remote(src.at[rows, pl.ds(col_src[slot], W)], colbuf.at[s, slot, n, rows, :], cs_s.at[s, slot, n, g], cs_r.at[s, slot, n, g], col_dev[slot])

    def above_copy(q):
        r0, nr, c0, nc = PIECES[q]
        return remote(m_ref.at[TR - W + r0 : TR - W + r0 + nr, c0 : c0 + nc], ext.at[r0 : r0 + nr, c0 : c0 + nc], ab_s.at[q], ab_r.at[q], (jnp.minimum(r + 1, ROWS - 1), c))

    def piece(ref, q, off=0):
        if isinstance(q, int) and q in LATE:
            r0, nr, c0, nc = PIECES[q]
            return ref.at[pl.ds(mult(off + r0, BS), nr), c0 : c0 + nc]
        return ref.at[pl.ds(mult(off + q * BS, BS), BS), :]

    def part(q):
        return 0 if isinstance(q, int) and q in LATE else q - 2

    def hops(q):
        return jnp.where(half == 1, dz - part(q) + 4, part(q) - dz + 4) % 4

    def goes_up(q):
        return jnp.where(near, dz < 2, (half == 1) & (hops(q) < 3))

    def goes_down(q):
        return jnp.where(near, dz == 0, (half == 0) & (hops(q) < 3))

    def goes_across(q):
        return near & (dz == part(q))

    def up_copy(q):
        return remote(piece(band, q), piece(band, q), up_s.at[q], bd_r.at[q], (z_up, c))

    def down_copy(q):
        return remote(piece(band, q), piece(band, q), dn_s.at[q], bd_r.at[q], (z_dn, c))

    def across_copy(q):
        return remote(piece(band, q), piece(band, q), cr_s.at[q], bd_r.at[q], (a_row, c))

    def forward(q):
        @pl.when(goes_across(q))
        def _():
            across_copy(q).start()

        @pl.when(goes_up(q))
        def _():
            up_copy(q).start()

        @pl.when(goes_down(q))
        def _():
            down_copy(q).start()

    def own_piece(q):
        src = piece(ext, q, ext_off) if q in LATE else piece(m_ref, q, ext_off - W)
        return pltpu.make_async_copy(src, piece(band, q), lsem.at[3 + q])

    barrier = pltpu.get_barrier_semaphore()

    def greet(dev):
        pl.semaphore_signal(barrier, inc=1, device_id=dev, device_id_type=MESH)

    for dev in (row_dev[0], col_dev[0], (z_up, c), (z_dn, c)):
        greet(dev)

    @pl.when(has_b)
    def _():
        greet(row_dev[1])

    @pl.when(has_y)
    def _():
        greet(col_dev[1])

    loads = [
        pltpu.make_async_copy(a_ref, dens.at[0], lsem.at[0]),
        pltpu.make_async_copy(b_ref, dens.at[1], lsem.at[1]),
        pltpu.make_async_copy(m_ref, ext.at[W:, :], lsem.at[2]),
    ]

    @pl.when(is_src)
    def _():
        for q in EARLY:
            own_piece(q).start()

    for cp in loads:
        cp.start()

    @pl.when(jnp.logical_not(first))
    def _():
        ext[0:W, :] = jnp.zeros((W, 3 * BS), F32)

    pl.semaphore_wait(barrier, 4 + has_b.astype(jnp.int32) + has_y.astype(jnp.int32))

    @pl.when(last)
    def _():
        for q in LATE:
            above_copy(q).start()

    row_copy(0, 0, 0).start()

    def start_rest():
        row_copy(0, 0, 1).start()

        @pl.when(has_b)
        def _():
            for n in range(2):
                row_copy(0, 1, n).start()

    @pl.when(jnp.logical_not(near))
    def _():
        start_rest()

    @pl.when(is_src)
    def _():
        for q in (4, 3, 5, 2):
            own_piece(q).wait()
            forward(q)

    def start_cols(s, g):
        for n in range(2):
            col_copy(s, 0, n, g).start()

        @pl.when(has_y)
        def _():
            for n in range(2):
                col_copy(s, 1, n, g).start()

    @pl.loop(0, NG)
    def _(t):
        start_cols(0, order(0, t))

    @pl.when(jnp.logical_not(has_b))
    def _():
        for s in range(2):
            for n in range(2):
                for p in range(2):
                    xs[s, n, p, pl.ds(row_dst[1], W), :] = jnp.zeros((W, TC + 2 * W), BF16)

    @pl.when(jnp.logical_not(has_y))
    def _():
        for s in range(2):
            for n in range(2):
                for p in range(2):
                    xs[s, n, p, :, pl.ds(col_dst[1], W)] = jnp.zeros((TR + 2 * W, W), BF16)

    loads[0].wait()
    loads[1].wait()

    @pl.loop(0, 2 * NG)
    def _(i):
        n, g = i // NG, i % NG
        hi, lo = split(dens[n, pl.ds(mult(g * W), W), :])
        xs[0, n, 0, pl.ds(mult(W + g * W), W), W : W + TC] = hi
        xs[0, n, 1, pl.ds(mult(W + g * W), W), W : W + TC] = lo

    loads[2].wait()

    @pl.when(is_src)
    def _():
        @pl.when(first)
        def _():
            for q in LATE:
                above_copy(q).wait_recv()

        for q in LATE:
            own_piece(q).start()
        for q in LATE:
            own_piece(q).wait()
            forward(q)
        start_rest()

    @pl.when(jnp.logical_not(is_src))
    def _():
        for e in range(4):
            q = 2 + jnp.where(near, (2, 1, 3, 0)[e], jnp.where(half == 1, dz - e + 4, dz + e) % 4)
            up_copy(q).wait_recv()
            forward(q)

            @pl.when(goes_across(q))
            def _():
                start_rest()

        @pl.when(first)
        def _():
            for q in LATE:
                above_copy(q).wait_recv()

    @pl.loop(0, TR // BS)
    def _(i):
        g, h = i // 2, i % 2
        rows = pl.ds(mult(h * BS, BS), BS)

        def put(pos, value):
            hi, lo = split(value * STEP_TIME)
            cols = pl.ds(mult(pos * BS, BS), BS)
            hrow[0, g, rows, cols] = hi
            hrow[1, g, rows, cols] = lo

        for d in range(-KB, KB + 1):
            u = ext[pl.ds(mult((i + KB + min(d, 0)) * BS, BS), BS), abs(d) * BS : (abs(d) + 1) * BS]
            value = u if d > 0 else u.T if d < 0 else 0.5 * (u + u.T)
            put(h + d + KB, value)
        put((1 - h) * (2 * KB + 1), jnp.zeros((BS, BS), F32))

    @pl.when(jnp.logical_not(is_src))
    def _():
        for q in LATE:
            up_copy(q).wait_recv()
            forward(q)

    @pl.loop(0, TC // BS)
    def _(i):
        j, h = i // 2, i % 2
        cols = pl.ds(mult(h * BS, BS), BS)

        def put(pos, value):
            hi, lo = split(value * -STEP_TIME)
            rows = pl.ds(mult(pos * BS, BS), BS)
            ncol[0, j, rows, cols] = hi
            ncol[1, j, rows, cols] = lo

        for d in range(-KB, KB + 1):
            u = band[pl.ds(mult((i + KB + min(d, 0)) * BS, BS), BS), abs(d) * BS : (abs(d) + 1) * BS]
            value = u if d < 0 else u.T if d > 0 else 0.5 * (u + u.T)
            put(h + d + KB, value)
        put((1 - h) * (2 * KB + 1), jnp.zeros((BS, BS), F32))

    def take_cols(s, slot, g):
        rows = pl.ds(mult(g * W), W)
        for n in range(2):
            col_copy(s, slot, n, g).wait_recv()
        for n in range(2):
            hi, lo = split(colbuf[s, slot, n, rows, :])
            xs[s, n, 0, pl.ds(mult(W + g * W), W), pl.ds(col_dst[slot], W)] = hi
            xs[s, n, 1, pl.ds(mult(W + g * W), W), pl.ds(col_dst[slot], W)] = lo

    def take_rows(s, slot):
        for n in range(2):
            row_copy(s, slot, n).wait_recv()
        for n in range(2):
            hi, lo = split(rowbuf[s, slot, n])
            xs[s, n, 0, pl.ds(row_dst[slot], W), W : W + TC] = hi
            xs[s, n, 1, pl.ds(row_dst[slot], W), W : W + TC] = lo

    def product(s, n, g, j):
        r0, c0 = mult(g * W), mult(j * W)
        hi, lo = xs.at[s, 1 - n, 0], xs.at[s, 1 - n, 1]
        row_h = hi[pl.ds(r0, 3 * W), pl.ds(mult(c0 + W), W)]
        row_l = lo[pl.ds(r0, 3 * W), pl.ds(mult(c0 + W), W)]
        col_h = hi[pl.ds(mult(r0 + W), W), pl.ds(c0, 3 * W)]
        col_l = lo[pl.ds(mult(r0 + W), W), pl.ds(c0, 3 * W)]
        h_h, h_l = hrow[0, g], hrow[1, g]
        n_h, n_l = ncol[0, j], ncol[1, j]
        lhs = jnp.concatenate([h_h, h_h, h_l, col_h, col_l, col_h], axis=1)
        rhs = jnp.concatenate([row_h, row_l, row_h, n_h, n_h, n_l], axis=0)
        total = jnp.dot(lhs, rhs, preferred_element_type=F32)
        return jnp.where(n == 0, 1.0, -1.0).astype(F32) * total

    def out_copy(n, g):
        rows = pl.ds(mult(g * W), W)
        return pltpu.make_async_copy(dens.at[n, rows, :], (oa_ref, ob_ref)[n].at[rows, :], osem.at[n, g])

    for s in range(2):

        @pl.loop(0, NG)
        def _(t):
            g = order(s, t)
            take_cols(s, 0, g)

            @pl.when(has_y)
            def _():
                take_cols(s, 1, g)

            @pl.when(t == 2 * s)
            def _():
                take_rows(s, 0)

            @pl.when((t == 3) & has_b)
            def _():
                take_rows(s, 1)

            @pl.loop(0, 2 * NJ)
            def _(i):
                n, j = i // NJ, i % NJ
                value = product(s, n, g, j)
                rows, cols = pl.ds(mult(g * W), W), pl.ds(mult(j * W), W)
                if s == 0:
                    grad[n, rows, cols] = value
                    hi, lo = split(value)
                    xs[1, n, 0, pl.ds(mult(W + g * W), W), pl.ds(mult(W + j * W), W)] = hi
                    xs[1, n, 1, pl.ds(mult(W + g * W), W), pl.ds(mult(W + j * W), W)] = lo
                else:
                    dens[n, rows, cols] = dens[n, rows, cols] + grad[n, rows, cols] + 0.5 * value

            if s == 0:

                @pl.when(t == 0)
                def _():
                    for n in range(2):
                        row_copy(1, 0, n).start()

                @pl.when((t == 3) & has_b)
                def _():
                    for n in range(2):
                        row_copy(1, 1, n).start()

                start_cols(1, g)
            else:
                for n in range(2):
                    out_copy(n, g).start()

    for s in range(2):
        for n in range(2):
            row_copy(s, 0, n).wait_send()

        @pl.when(has_b)
        def _():
            for n in range(2):
                row_copy(s, 1, n).wait_send()

        @pl.loop(0, NG)
        def _(g):
            for n in range(2):
                col_copy(s, 0, n, g).wait_send()

            @pl.when(has_y)
            def _():
                for n in range(2):
                    col_copy(s, 1, n, g).wait_send()

    @pl.when(last)
    def _():
        for q in LATE:
            above_copy(q).wait_send()

    for q in range(6):

        @pl.when(goes_across(q))
        def _():
            across_copy(q).wait_send()

        @pl.when(goes_up(q))
        def _():
            up_copy(q).wait_send()

        @pl.when(goes_down(q))
        def _():
            down_copy(q).wait_send()

    @pl.loop(0, NG)
    def _(g):
        for n in range(2):
            out_copy(n, g).wait()


def masked_band(upper_band, pattern, first_block):
    block_count = pattern.shape[0]
    blocks = upper_band.reshape(block_count, BS, KB + 1, BS)
    block_index = first_block + jnp.arange(block_count, dtype=jnp.int32)
    offsets = jnp.arange(1, KB + 1, dtype=jnp.int32)
    present = (pattern > 0) & (block_index[:, None] + offsets[None, :] < NB)
    present = jnp.concatenate([jnp.ones((block_count, 1), bool), present], axis=1)
    lanes = jnp.repeat(present, BS, axis=1)
    rows = jnp.repeat(lanes, BS, axis=0)
    return jnp.where(rows, upper_band, 0.0)


def shards(dens_real, dens_imag, upper_band, pattern):
    first_block = lax.axis_index("row") * (TR // BS)
    masked = masked_band(upper_band, pattern, first_block)
    dma = pltpu.SemaphoreType.DMA
    anywhere = pl.BlockSpec(memory_space=pl.ANY)
    return pl.pallas_call(
        kernel,
        out_shape=(jax.ShapeDtypeStruct((TR, TC), F32),) * 2,
        in_specs=[anywhere] * 3,
        out_specs=(anywhere,) * 2,
        scratch_shapes=[
            pltpu.VMEM((2, TR, TC), F32),
            pltpu.VMEM((2, TR, TC), F32),
            pltpu.VMEM((2, 2, 2, TR + 2 * W, TC + 2 * W), BF16),
            pltpu.VMEM((2, 2, 2, W, TC), F32),
            pltpu.VMEM((2, 2, 2, TR, W), F32),
            pltpu.VMEM((TR + W, 3 * BS), F32),
            pltpu.VMEM((TC + W, 3 * BS), F32),
            pltpu.VMEM((2, NG, W, 3 * W), BF16),
            pltpu.VMEM((2, NJ, 3 * W, W), BF16),
            dma((9,)),
            dma((2, NG)),
            dma((2, 2, 2)),
            dma((2, 2, 2)),
            dma((2, 2, 2, NG)),
            dma((2, 2, 2, NG)),
            dma((2,)),
            dma((2,)),
            dma((6,)),
            dma((6,)),
            dma((6,)),
            dma((6,)),
        ],
        compiler_params=pltpu.CompilerParams(collective_id=0, has_side_effects=True, vmem_limit_bytes=63 << 20),
        name="heun",
    )(dens_real, dens_imag, masked)


def solution(mesh):
    in_specs = (P("row", "col"), P("row", "col"), P("row", None), P("row", None))
    out_specs = (P("row", "col"), P("row", "col"))
    return jax.shard_map(shards, mesh=mesh, in_specs=in_specs, out_specs=out_specs, check_vma=False)
```

```python
import jax
import jax.numpy as jnp
from jax import lax
from jax.experimental import pallas as pl
from jax.experimental.pallas import tpu as pltpu
from jax.sharding import PartitionSpec as P

BS = 128
KB = 2
NB = 64
STEP_TIME = 0.3
MESH = pl.DeviceIdType.MESH
F32 = jnp.float32
BF16 = jnp.bfloat16
TR = 1024
TC = 512
W = KB * BS
NG = TR // W
NJ = TC // W
ROWS = 8
COLS = 16
PIECES = [(0, BS, 2 * BS, BS), (BS, BS, BS, 2 * BS)] + [(q * BS, BS, 0, 3 * BS) for q in range(2, 6)]
LATE = (0, 1)
EARLY = (2, 3, 4, 5)


def mult(x, n=W):
    return pl.multiple_of(x, n)


def split(x):
    hi = x.astype(BF16)
    return hi, (x - hi.astype(F32)).astype(BF16)


def kernel(a_ref, b_ref, u_ref, pat_ref, dens, grad, xs, rowbuf, colbuf, ext, band, hrow, ncol, relay,
           lsem, rs_s, rs_r, cs_s, cs_r, ab_s, ab_r, up_s, dn_s, cr_s, bd_r, rl_s, rl_r):
    r, c = lax.axis_index("row"), lax.axis_index("col")
    even, core = r % 2 == 0, c % 2
    k = c // 2
    z, zk, half = r // 2, k // 2, r % 2
    dz = (z - zk + 4) % 4
    is_src = r == k
    near = half == k % 2
    a_row = jnp.where(even, r + 1, r - 1)
    b_row = jnp.where(even, r - 1, r + 1)
    has_b = (b_row >= 0) & (b_row < ROWS)
    cc_col = jnp.where(core == 0, c + 1, c - 1)
    cy_col = jnp.where(core == 0, c - 1, c + 1)
    has_y = (cy_col >= 0) & (cy_col < COLS)
    hub = (c == 7) | (c == 8)
    mine = jnp.minimum(c, COLS - 1 - c)
    is_relay = (mine % 2 == 0) & (mine < 6)
    relay_turn = jnp.where(mine == 0, 1, jnp.where(mine == 4, 2, 3))
    relay_to = jnp.where(c < 8, 8, 7)
    z_up, z_dn = (r + 2) % ROWS, (r + 6) % ROWS
    first = r > 0
    last = r < ROWS - 1

    row_dev = ((a_row, c), (b_row, c))
    row_src = (mult(jnp.where(even, TR - W, 0)), mult(jnp.where(even, 0, TR - W)))
    row_dst = (mult(jnp.where(even, TR + W, 0)), mult(jnp.where(even, 0, TR + W)))
    col_dev = ((r, cc_col), (r, cy_col))
    col_src = (mult(jnp.where(core == 0, TC - W, 0)), mult(jnp.where(core == 0, 0, TC - W)))
    col_dst = (mult(jnp.where(core == 0, TC + W, 0)), mult(jnp.where(core == 0, 0, TC + W)))
    g_a = jnp.where(even, NG - 1, 0)
    ext_off = mult(core * TC, BS)

    def order(s, t):
        if s == 0:
            return jnp.where(t == 0, g_a, jnp.where(t == 3, NG - 1 - g_a, t))
        return jnp.where(t < 2, t + 1, jnp.where(t == 2, g_a, NG - 1 - g_a))

    def remote(src, dst, ss, rs, dev):
        return pltpu.make_async_remote_copy(src, dst, ss, rs, device_id=dev, device_id_type=MESH)

    def row_copy(s, slot, n):
        src = (a_ref, b_ref)[n] if s == 0 else grad.at[n]
        return remote(src.at[pl.ds(row_src[slot], W), :], rowbuf.at[s, slot, n], rs_s.at[s, slot, n], rs_r.at[s, slot, n], row_dev[slot])

    def col_copy(s, slot, n, g):
        src = (a_ref, b_ref)[n] if s == 0 else grad.at[n]
        rows = pl.ds(mult(g * W), W)
        return remote(src.at[rows, pl.ds(col_src[slot], W)], colbuf.at[s, slot, n, rows, :], cs_s.at[s, slot, n, g], cs_r.at[s, slot, n, g], col_dev[slot])

    def hub_copy(s, n, t):
        g = order(0, t)
        src = (a_ref, b_ref)[n] if s == 0 else grad.at[n]
        near_col = jnp.where(t == 1, 0, jnp.where(t == 2, 4, 2))
        to = jnp.where(c < 8, near_col, COLS - 1 - near_col)
        return remote(src.at[pl.ds(mult(g * W), W), pl.ds(col_src[1], W)], relay.at[s, n], cs_s.at[s, 1, n, g], rl_r.at[s, n], (r, to))

    def relay_copy(s, n):
        g = order(0, relay_turn)
        return remote(relay.at[s, n], colbuf.at[s, 1, n, pl.ds(mult(g * W), W), :], rl_s.at[s, n], cs_r.at[s, 1, n, g], (r, relay_to))

    def pass_on(s):
        @pl.when(is_relay)
        def _():
            for n in range(2):
                hub_copy(s, n, 1).wait_recv()
            for n in range(2):
                relay_copy(s, n).start()

    def above_copy(q):
        r0, nr, c0, nc = PIECES[q]
        return remote(ext.at[TR + r0 : TR + r0 + nr, c0 : c0 + nc], ext.at[r0 : r0 + nr, c0 : c0 + nc], ab_s.at[q], ab_r.at[q], (jnp.minimum(r + 1, ROWS - 1), c))

    def piece(ref, q, off=0):
        if isinstance(q, int) and q in LATE:
            r0, nr, c0, nc = PIECES[q]
            return ref.at[pl.ds(mult(off + r0, BS), nr), c0 : c0 + nc]
        return ref.at[pl.ds(mult(off + q * BS, BS), BS), :]

    def part(q):
        return 0 if isinstance(q, int) and q in LATE else q - 2

    def hops(q):
        return jnp.where(half == 1, dz - part(q) + 4, part(q) - dz + 4) % 4

    def goes_up(q):
        return jnp.where(near, dz < 2, (half == 1) & (hops(q) < 3))

    def goes_down(q):
        return jnp.where(near, dz == 0, (half == 0) & (hops(q) < 3))

    def goes_across(q):
        return near & (dz == part(q))

    def up_copy(q):
        return remote(piece(band, q), piece(band, q), up_s.at[q], bd_r.at[q], (z_up, c))

    def down_copy(q):
        return remote(piece(band, q), piece(band, q), dn_s.at[q], bd_r.at[q], (z_dn, c))

    def across_copy(q):
        return remote(piece(band, q), piece(band, q), cr_s.at[q], bd_r.at[q], (a_row, c))

    def forward(q):
        @pl.when(goes_across(q))
        def _():
            across_copy(q).start()

        @pl.when(goes_up(q))
        def _():
            up_copy(q).start()

        @pl.when(goes_down(q))
        def _():
            down_copy(q).start()

    def own_piece(q):
        return pltpu.make_async_copy(piece(ext, q, ext_off), piece(band, q), lsem.at[3 + q])

    barrier = pltpu.get_barrier_semaphore()

    def greet(dev):
        pl.semaphore_signal(barrier, inc=1, device_id=dev, device_id_type=MESH)

    for dev in (row_dev[0], col_dev[0], (z_up, c), (z_dn, c)):
        greet(dev)

    @pl.when(has_b)
    def _():
        greet(row_dev[1])

    @pl.when(has_y)
    def _():
        greet(col_dev[1])

    loads = [
        pltpu.make_async_copy(a_ref, dens.at[0], lsem.at[0]),
        pltpu.make_async_copy(b_ref, dens.at[1], lsem.at[1]),
        pltpu.make_async_copy(u_ref, ext.at[W:, :], lsem.at[2]),
    ]

    for cp in loads[::-1]:
        cp.start()

    @pl.when(jnp.logical_not(first))
    def _():
        ext[0:W, :] = jnp.zeros((W, 3 * BS), F32)

    loads[2].wait()

    @pl.loop(0, TR // BS)
    def _(i):
        rows = pl.ds(mult(W + i * BS, BS), BS)
        for d in range(1, KB + 1):
            present = (pat_ref[i, d - 1] > 0) & (r * (TR // BS) + i + d < NB)
            cols = slice(d * BS, (d + 1) * BS)
            ext[rows, cols] = ext[rows, cols] * jnp.where(present, 1.0, 0.0).astype(F32)

    @pl.when(is_src)
    def _():
        for q in EARLY:
            own_piece(q).start()

    @pl.when(hub)
    def _():
        for col in (0, 2, 4, 11, 13, 15):
            greet((r, col))

    @pl.when(is_relay)
    def _():
        for col in (7, 8):
            greet((r, col))

    pl.semaphore_wait(barrier, 4 + has_b.astype(jnp.int32) + has_y.astype(jnp.int32) + jnp.where(hub, 6, 0) + jnp.where(is_relay, 2, 0))

    @pl.when(last)
    def _():
        for q in LATE:
            above_copy(q).start()

    row_copy(0, 0, 0).start()

    def start_b():
        pass_on(0)

        @pl.when(has_b)
        def _():
            for n in range(2):
                row_copy(0, 1, n).start()

    @pl.when(jnp.logical_not(near))
    def _():
        row_copy(0, 0, 1).start()

    @pl.when(is_src)
    def _():
        for q in (4, 3, 5, 2):
            own_piece(q).wait()
            forward(q)

    def start_cols(s, t):
        g = order(0, t)
        for n in range(2):
            col_copy(s, 0, n, g).start()

        @pl.when(has_y & (jnp.logical_not(hub) | (t == 0)))
        def _():
            for n in range(2):
                col_copy(s, 1, n, g).start()

        @pl.when(hub & (t > 0))
        def _():
            for n in range(2):
                hub_copy(s, n, t).start()

    @pl.loop(0, NG)
    def _(t):
        start_cols(0, t)

    def clear_rows(s):
        for n in range(2):
            for p in range(2):
                xs[s, n, p, pl.ds(row_dst[1], W), W : W + TC] = jnp.zeros((W, TC), BF16)

    @pl.when(jnp.logical_not(has_b))
    def _():
        clear_rows(0)

    clear_rows(1)

    @pl.when(jnp.logical_not(has_y))
    def _():
        for s in range(2):
            for n in range(2):
                for p in range(2):
                    xs[s, n, p, :, pl.ds(col_dst[1], W)] = jnp.zeros((TR + 2 * W, W), BF16)

    loads[0].wait()
    loads[1].wait()

    @pl.loop(0, 2 * NG)
    def _(i):
        n, g = i // NG, i % NG
        hi, lo = split(dens[n, pl.ds(mult(g * W), W), :])
        xs[0, n, 0, pl.ds(mult(W + g * W), W), W : W + TC] = hi
        xs[0, n, 1, pl.ds(mult(W + g * W), W), W : W + TC] = lo

    @pl.when(is_src)
    def _():
        @pl.when(first)
        def _():
            for q in LATE:
                above_copy(q).wait_recv()

        for q in LATE:
            own_piece(q).start()
        for q in LATE:
            own_piece(q).wait()
            forward(q)
        row_copy(0, 0, 1).start()
        start_b()

    @pl.when(jnp.logical_not(near))
    def _():
        start_b()

    @pl.when(jnp.logical_not(is_src))
    def _():
        for e in range(4):
            q = 2 + jnp.where(near, (2, 1, 3, 0)[e], jnp.where(half == 1, dz - e + 4, dz + e) % 4)
            up_copy(q).wait_recv()
            forward(q)

            @pl.when(goes_across(q))
            def _():
                row_copy(0, 0, 1).start()

            if e == 2:

                @pl.when(near)
                def _():
                    start_b()

        @pl.when(first)
        def _():
            for q in LATE:
                above_copy(q).wait_recv()

    @pl.loop(0, TR // BS)
    def _(i):
        g, h = i // 2, i % 2
        rows = pl.ds(mult(h * BS, BS), BS)

        def put(pos, value):
            hi, lo = split(value * STEP_TIME)
            cols = pl.ds(mult(pos * BS, BS), BS)
            hrow[0, g, rows, cols] = hi
            hrow[1, g, rows, cols] = lo

        for d in range(-KB, KB + 1):
            u = ext[pl.ds(mult((i + KB + min(d, 0)) * BS, BS), BS), abs(d) * BS : (abs(d) + 1) * BS]
            value = u if d > 0 else u.T if d < 0 else 0.5 * (u + u.T)
            put(h + d + KB, value)
        put((1 - h) * (2 * KB + 1), jnp.zeros((BS, BS), F32))

    @pl.when(jnp.logical_not(is_src))
    def _():
        for q in LATE:
            up_copy(q).wait_recv()
            forward(q)

    @pl.loop(0, TC // BS)
    def _(i):
        j, h = i // 2, i % 2
        cols = pl.ds(mult(h * BS, BS), BS)

        def put(pos, value):
            hi, lo = split(value * -STEP_TIME)
            rows = pl.ds(mult(pos * BS, BS), BS)
            ncol[0, j, rows, cols] = hi
            ncol[1, j, rows, cols] = lo

        for d in range(-KB, KB + 1):
            u = band[pl.ds(mult((i + KB + min(d, 0)) * BS, BS), BS), abs(d) * BS : (abs(d) + 1) * BS]
            value = u if d < 0 else u.T if d > 0 else 0.5 * (u + u.T)
            put(h + d + KB, value)
        put((1 - h) * (2 * KB + 1), jnp.zeros((BS, BS), F32))

    def take_cols(s, slot, g):
        rows = pl.ds(mult(g * W), W)
        for n in range(2):
            col_copy(s, slot, n, g).wait_recv()
        for n in range(2):
            hi, lo = split(colbuf[s, slot, n, rows, :])
            xs[s, n, 0, pl.ds(mult(W + g * W), W), pl.ds(col_dst[slot], W)] = hi
            xs[s, n, 1, pl.ds(mult(W + g * W), W), pl.ds(col_dst[slot], W)] = lo

    def take_rows(s, slot):
        for n in range(2):
            row_copy(s, slot, n).wait_recv()
        for n in range(2):
            hi, lo = split(rowbuf[s, slot, n])
            xs[s, n, 0, pl.ds(row_dst[slot], W), W : W + TC] = hi
            xs[s, n, 1, pl.ds(row_dst[slot], W), W : W + TC] = lo

    def product(s, n, g, j):
        r0, c0 = mult(g * W), mult(j * W)
        hi, lo = xs.at[s, 1 - n, 0], xs.at[s, 1 - n, 1]
        row_h = hi[pl.ds(r0, 3 * W), pl.ds(mult(c0 + W), W)]
        row_l = lo[pl.ds(r0, 3 * W), pl.ds(mult(c0 + W), W)]
        col_h = hi[pl.ds(mult(r0 + W), W), pl.ds(c0, 3 * W)]
        col_l = lo[pl.ds(mult(r0 + W), W), pl.ds(c0, 3 * W)]
        h_h, h_l = hrow[0, g], hrow[1, g]
        n_h, n_l = ncol[0, j], ncol[1, j]
        lhs = jnp.concatenate([h_h, h_h, h_l, col_h, col_l, col_h], axis=1)
        rhs = jnp.concatenate([row_h, row_l, row_h, n_h, n_h, n_l], axis=0)
        total = jnp.dot(lhs, rhs, preferred_element_type=F32)
        return jnp.where(n == 0, 1.0, -1.0).astype(F32) * total

    def last_part(n):
        g = NG - 1 - g_a
        row_copy(1, 1, n).wait_recv()
        hi, lo = split(rowbuf[1, 1, n])
        cols = pl.ds(mult(jnp.where(even, 0, 2 * W)), W)
        h_h, h_l = hrow[0, g, :, cols], hrow[1, g, :, cols]
        lhs = jnp.concatenate([h_h, h_h, h_l], axis=1)
        rhs = jnp.concatenate([hi, lo, hi], axis=0)
        rows = pl.ds(mult(g * W), W)
        dens[1 - n, rows, :] += (-0.5 if n == 0 else 0.5) * jnp.dot(lhs, rhs, preferred_element_type=F32)

    for s in range(2):

        @pl.loop(0, NG)
        def _(t):
            g = order(s, t)
            take_cols(s, 0, g)

            @pl.when(has_y)
            def _():
                take_cols(s, 1, g)

            @pl.when(t == 2 * s)
            def _():
                take_rows(s, 0)

            if s == 0:

                @pl.when((t == 3) & has_b)
                def _():
                    take_rows(s, 1)

            @pl.loop(0, 2 * NJ)
            def _(i):
                n, j = i // NJ, i % NJ
                value = product(s, n, g, j)
                rows, cols = pl.ds(mult(g * W), W), pl.ds(mult(j * W), W)
                if s == 0:
                    grad[n, rows, cols] = value
                    hi, lo = split(value)
                    xs[1, n, 0, pl.ds(mult(W + g * W), W), pl.ds(mult(W + j * W), W)] = hi
                    xs[1, n, 1, pl.ds(mult(W + g * W), W), pl.ds(mult(W + j * W), W)] = lo
                else:
                    dens[n, rows, cols] = dens[n, rows, cols] + grad[n, rows, cols] + 0.5 * value

            if s == 0:

                @pl.when(t == 0)
                def _():
                    for n in range(2):
                        row_copy(1, 0, n).start()

                start_cols(1, t)

                @pl.when(t == 3)
                def _():
                    pass_on(1)

                @pl.when((t == 3) & has_b)
                def _():
                    for n in range(2):
                        row_copy(1, 1, n).start()

    @pl.when(has_b)
    def _():
        for n in range(2):
            last_part(n)

    for s in range(2):
        for n in range(2):
            row_copy(s, 0, n).wait_send()

        @pl.when(has_b)
        def _():
            for n in range(2):
                row_copy(s, 1, n).wait_send()

        @pl.loop(0, NG)
        def _(g):
            for n in range(2):
                col_copy(s, 0, n, g).wait_send()

            @pl.when(has_y)
            def _():
                for n in range(2):
                    col_copy(s, 1, n, g).wait_send()

    @pl.when(is_relay)
    def _():
        for s in range(2):
            for n in range(2):
                relay_copy(s, n).wait_send()

    @pl.when(last)
    def _():
        for q in LATE:
            above_copy(q).wait_send()

    for q in range(6):

        @pl.when(goes_across(q))
        def _():
            across_copy(q).wait_send()

        @pl.when(goes_up(q))
        def _():
            up_copy(q).wait_send()

        @pl.when(goes_down(q))
        def _():
            down_copy(q).wait_send()


def shards(dens_real, dens_imag, upper_band, pattern):
    dma = pltpu.SemaphoreType.DMA
    anywhere = pl.BlockSpec(memory_space=pl.ANY)
    out = pl.pallas_call(
        kernel,
        out_shape=pltpu.VMEM((2, TR, TC), F32),
        in_specs=[anywhere] * 3 + [pl.BlockSpec(memory_space=pltpu.SMEM)],
        out_specs=pl.BlockSpec(memory_space=pltpu.VMEM),
        scratch_shapes=[
            pltpu.VMEM((2, TR, TC), F32),
            pltpu.VMEM((2, 2, 2, TR + 2 * W, TC + 2 * W), BF16),
            pltpu.VMEM((2, 2, 2, W, TC), F32),
            pltpu.VMEM((2, 2, 2, TR, W), F32),
            pltpu.VMEM((TR + W, 3 * BS), F32),
            pltpu.VMEM((TC + W, 3 * BS), F32),
            pltpu.VMEM((2, NG, W, 3 * W), BF16),
            pltpu.VMEM((2, NJ, 3 * W, W), BF16),
            pltpu.VMEM((2, 2, W, W), F32),
            dma((9,)),
            dma((2, 2, 2)),
            dma((2, 2, 2)),
            dma((2, 2, 2, NG)),
            dma((2, 2, 2, NG)),
            dma((2,)),
            dma((2,)),
            dma((6,)),
            dma((6,)),
            dma((6,)),
            dma((6,)),
            dma((2, 2)),
            dma((2, 2)),
        ],
        compiler_params=pltpu.CompilerParams(collective_id=0, has_side_effects=True, vmem_limit_bytes=55 << 20),
        name="heun",
    )(dens_real, dens_imag, upper_band, pattern)
    return out[0], out[1]


def solution(mesh):
    in_specs = (P("row", "col"), P("row", "col"), P("row", None), P("row", None))
    out_specs = (P("row", "col"), P("row", "col"))
    return jax.shard_map(shards, mesh=mesh, in_specs=in_specs, out_specs=out_specs, check_vma=False)
```

```python
import jax
import jax.numpy as jnp
from jax import lax
from jax.experimental import pallas as pl
from jax.experimental.pallas import tpu as pltpu
from jax.sharding import PartitionSpec as P

BS = 128
KB = 2
NB = 64
STEP_TIME = 0.3
MESH = pl.DeviceIdType.MESH
F32 = jnp.float32
BF16 = jnp.bfloat16
TR = 1024
TC = 512
W = KB * BS
NG = TR // W
NJ = TC // W
ROWS = 8
COLS = 16
PIECES = [(0, BS, 2 * BS, BS), (BS, BS, BS, 2 * BS)] + [(q * BS, BS, 0, 3 * BS) for q in range(2, 6)]
LATE = (0, 1)
EARLY = (2, 3, 4, 5)


def mult(x, n=W):
    return pl.multiple_of(x, n)


def split(x):
    hi = x.astype(BF16)
    return hi, (x - hi.astype(F32)).astype(BF16)


def kernel(a_ref, b_ref, u_ref, pat_ref, dens, grad, xs, rowbuf, colbuf, ext, band, hrow, ncol, relay, zrelay,
           lsem, rs_s, rs_r, bs_s, bs_r, bz_s, bz_r, cs_s, cs_r, ab_s, ab_r, al_s, cr_s, bd_r, rl_s, rl_r):
    r, c = lax.axis_index("row"), lax.axis_index("col")
    even, core = r % 2 == 0, c % 2
    k = c // 2
    z, zk, half = r // 2, k // 2, r % 2
    step_up = k % 2 == 0
    dist = jnp.where(step_up, z - zk, zk - z)
    dist = (dist + 4) % 4
    is_src = r == k
    near = half == k % 2
    a_row = jnp.where(even, r + 1, r - 1)
    b_row = jnp.where(even, r - 1, r + 1)
    has_b = (b_row >= 0) & (b_row < ROWS)
    cc_col = jnp.where(core == 0, c + 1, c - 1)
    cy_col = jnp.where(core == 0, c - 1, c + 1)
    has_y = (cy_col >= 0) & (cy_col < COLS)
    hub = (c == 7) | (c == 8)
    mine = jnp.minimum(c, COLS - 1 - c)
    is_relay = (mine % 2 == 0) & (mine < 6)
    relay_turn = jnp.where(mine == 0, 1, jnp.where(mine == 4, 2, 3))
    relay_to = jnp.where(c < 8, 8, 7)
    z_up, z_dn = (r + 2) % ROWS, (r + 6) % ROWS
    z_next = jnp.where(step_up, z_up, z_dn)
    depth = jnp.where(even, z, 3 - z)
    first_far = depth
    z_relay = jnp.where(even, z_dn, z_up)
    first = r > 0
    last = r < ROWS - 1

    row_dev = ((a_row, c), (b_row, c))
    row_src = (mult(jnp.where(even, TR - W, 0)), mult(jnp.where(even, 0, TR - W)))
    row_dst = (mult(jnp.where(even, TR + W, 0)), mult(jnp.where(even, 0, TR + W)))
    col_dev = ((r, cc_col), (r, cy_col))
    col_src = (mult(jnp.where(core == 0, TC - W, 0)), mult(jnp.where(core == 0, 0, TC - W)))
    col_dst = (mult(jnp.where(core == 0, TC + W, 0)), mult(jnp.where(core == 0, 0, TC + W)))
    g_a = jnp.where(even, NG - 1, 0)
    ext_off = mult(core * TC, BS)

    def order(s, t):
        if s == 0:
            return jnp.where(t == 0, g_a, jnp.where(t == 3, NG - 1 - g_a, t))
        return jnp.where(t < 2, t + 1, jnp.where(t == 2, g_a, NG - 1 - g_a))

    def remote(src, dst, ss, rs, dev):
        return pltpu.make_async_remote_copy(src, dst, ss, rs, device_id=dev, device_id_type=MESH)

    def row_copy(s, n):
        src = (a_ref, b_ref)[n] if s == 0 else grad.at[n]
        return remote(src.at[pl.ds(row_src[0], W), :], rowbuf.at[s, 0, n], rs_s.at[s, n], rs_r.at[s, n], row_dev[0])

    def b_src(s, i):
        src = (a_ref, b_ref)[i // 2] if s == 0 else grad.at[i // 2]
        return src.at[pl.ds(mult(row_src[1] + i % 2 * BS, BS), BS), :]

    def b_dst(s, i):
        return rowbuf.at[s, 1, i // 2, i % 2 * BS : (i % 2 + 1) * BS, :]

    def b_direct(s, i):
        return remote(b_src(s, i), b_dst(s, i), bs_s.at[s, i], bs_r.at[s, i], row_dev[1])

    def b_first(s, i):
        return remote(b_src(s, i), zrelay.at[s, i], bs_s.at[s, i], bz_r.at[s, i], (z_relay, c))

    def b_second(s, i):
        return remote(zrelay.at[s, i], b_dst(s, i), bz_s.at[s, i], bs_r.at[s, i], (a_row, c))

    def b_far(s):
        for i in range(4):

            @pl.when(has_b & (i >= first_far))
            def _():
                b_first(s, i).start()

    def b_near(s):
        for i in range(3):

            @pl.when(has_b & (i < first_far))
            def _():
                b_direct(s, i).start()

    def b_pass(s):
        for i in range(1, 4):

            @pl.when(i > depth)
            def _():
                b_first(s, i).wait_recv()
                b_second(s, i).start()

    def col_copy(s, slot, n, g):
        src = (a_ref, b_ref)[n] if s == 0 else grad.at[n]
        rows = pl.ds(mult(g * W), W)
        return remote(src.at[rows, pl.ds(col_src[slot], W)], colbuf.at[s, slot, n, rows, :], cs_s.at[s, slot, n, g], cs_r.at[s, slot, n, g], col_dev[slot])

    def hub_copy(s, n, t):
        g = order(0, t)
        src = (a_ref, b_ref)[n] if s == 0 else grad.at[n]
        near_col = jnp.where(t == 1, 0, jnp.where(t == 2, 4, 2))
        to = jnp.where(c < 8, near_col, COLS - 1 - near_col)
        return remote(src.at[pl.ds(mult(g * W), W), pl.ds(col_src[1], W)], relay.at[s, n], cs_s.at[s, 1, n, g], rl_r.at[s, n], (r, to))

    def relay_copy(s, n):
        g = order(0, relay_turn)
        return remote(relay.at[s, n], colbuf.at[s, 1, n, pl.ds(mult(g * W), W), :], rl_s.at[s, n], cs_r.at[s, 1, n, g], (r, relay_to))

    def pass_on(s, turns):
        @pl.when(is_relay & ((relay_turn == 3) == (turns == 3)))
        def _():
            for n in range(2):
                hub_copy(s, n, 1).wait_recv()
            for n in range(2):
                relay_copy(s, n).start()

    def above_copy(q):
        r0, nr, c0, nc = PIECES[q]
        return remote(ext.at[TR + r0 : TR + r0 + nr, c0 : c0 + nc], ext.at[r0 : r0 + nr, c0 : c0 + nc], ab_s.at[q], ab_r.at[q], (jnp.minimum(r + 1, ROWS - 1), c))

    def piece(ref, q, off=0):
        if isinstance(q, int) and q in LATE:
            r0, nr, c0, nc = PIECES[q]
            return ref.at[pl.ds(mult(off + r0, BS), nr), c0 : c0 + nc]
        return ref.at[pl.ds(mult(off + q * BS, BS), BS), :]

    def part(q):
        return 0 if isinstance(q, int) and q in LATE else q - 2

    def hops(q):
        return (dist - part(q) + 4) % 4

    def goes_along(q):
        return jnp.where(near, dist, hops(q)) < 3

    def goes_across(q):
        return near & (dist == part(q))

    def along_copy(q):
        return remote(piece(band, q), piece(band, q), al_s.at[q], bd_r.at[q], (z_next, c))

    def across_copy(q):
        return remote(piece(band, q), piece(band, q), cr_s.at[q], bd_r.at[q], (a_row, c))

    def along(q):
        @pl.when(goes_along(q))
        def _():
            along_copy(q).start()

    def forward(q):
        @pl.when(goes_across(q))
        def _():
            across_copy(q).start()

        along(q)

    def own_piece(q):
        return pltpu.make_async_copy(piece(ext, q, ext_off), piece(band, q), lsem.at[3 + q])

    barrier = pltpu.get_barrier_semaphore()

    def greet(dev):
        pl.semaphore_signal(barrier, inc=1, device_id=dev, device_id_type=MESH)

    for dev in (row_dev[0], col_dev[0], (z_up, c), (z_dn, c)):
        greet(dev)

    @pl.when(has_b)
    def _():
        greet(row_dev[1])

    @pl.when(has_y)
    def _():
        greet(col_dev[1])

    loads = [
        pltpu.make_async_copy(a_ref, dens.at[0], lsem.at[0]),
        pltpu.make_async_copy(b_ref, dens.at[1], lsem.at[1]),
        pltpu.make_async_copy(u_ref, ext.at[W:, :], lsem.at[2]),
    ]

    for cp in loads[::-1]:
        cp.start()

    @pl.when(jnp.logical_not(first))
    def _():
        ext[0:W, :] = jnp.zeros((W, 3 * BS), F32)

    loads[2].wait()

    @pl.loop(0, TR // BS)
    def _(i):
        rows = pl.ds(mult(W + i * BS, BS), BS)
        for d in range(1, KB + 1):
            present = (pat_ref[i, d - 1] > 0) & (r * (TR // BS) + i + d < NB)
            cols = slice(d * BS, (d + 1) * BS)
            ext[rows, cols] = ext[rows, cols] * jnp.where(present, 1.0, 0.0).astype(F32)

    @pl.when(is_src)
    def _():
        for q in EARLY:
            own_piece(q).start()

    @pl.when(hub)
    def _():
        for col in (0, 2, 4, 11, 13, 15):
            greet((r, col))

    @pl.when(is_relay)
    def _():
        for col in (7, 8):
            greet((r, col))

    pl.semaphore_wait(barrier, 4 + has_b.astype(jnp.int32) + has_y.astype(jnp.int32) + jnp.where(hub, 6, 0) + jnp.where(is_relay, 2, 0))

    @pl.when(last)
    def _():
        for q in LATE:
            above_copy(q).start()

    def start_b():
        pass_on(0, 1)
        b_near(0)
        b_pass(0)

    @pl.when(is_src)
    def _():
        own_piece(2).wait()
        across_copy(2).start()

    row_copy(0, 0).start()

    @pl.when(jnp.logical_not(near))
    def _():
        row_copy(0, 1).start()

    b_far(0)

    @pl.when(is_src)
    def _():
        for q in (5, 4, 3):
            own_piece(q).wait()
            along(q)
        along(2)

    def start_cols(s, t):
        g = order(0, t)
        for n in range(2):
            col_copy(s, 0, n, g).start()

        @pl.when(has_y & (jnp.logical_not(hub) | (t == 0)))
        def _():
            for n in range(2):
                col_copy(s, 1, n, g).start()

        @pl.when(hub & (t > 0))
        def _():
            for n in range(2):
                hub_copy(s, n, t).start()

    @pl.loop(0, NG)
    def _(t):
        start_cols(0, t)

    def clear_rows(s):
        for n in range(2):
            for p in range(2):
                xs[s, n, p, pl.ds(row_dst[1], W), W : W + TC] = jnp.zeros((W, TC), BF16)

    @pl.when(jnp.logical_not(has_b))
    def _():
        clear_rows(0)

    clear_rows(1)

    @pl.when(jnp.logical_not(has_y))
    def _():
        for s in range(2):
            for n in range(2):
                for p in range(2):
                    xs[s, n, p, :, pl.ds(col_dst[1], W)] = jnp.zeros((TR + 2 * W, W), BF16)

    loads[0].wait()
    loads[1].wait()

    @pl.loop(0, 2 * NG)
    def _(i):
        n, g = i // NG, i % NG
        hi, lo = split(dens[n, pl.ds(mult(g * W), W), :])
        xs[0, n, 0, pl.ds(mult(W + g * W), W), W : W + TC] = hi
        xs[0, n, 1, pl.ds(mult(W + g * W), W), W : W + TC] = lo

    @pl.when(is_src)
    def _():
        @pl.when(first)
        def _():
            for q in LATE:
                above_copy(q).wait_recv()

        for q in LATE:
            own_piece(q).start()
        for q in LATE:
            own_piece(q).wait()
            forward(q)
        row_copy(0, 1).start()
        start_b()

    @pl.when(jnp.logical_not(is_src))
    def _():
        for e in range(4):
            q = 2 + jnp.where(near, 3 - e, (dist - e + 4) % 4)
            along_copy(q).wait_recv()
            forward(q)

            @pl.when(goes_across(q))
            def _():
                row_copy(0, 1).start()

            @pl.when(e == jnp.where(near, 2, 0))
            def _():
                start_b()

            @pl.when(e == jnp.where(near, 3, dist))
            def _():
                for p in LATE:
                    along_copy(p).wait_recv()
                    forward(p)

        @pl.when(first)
        def _():
            for q in LATE:
                above_copy(q).wait_recv()

    pass_on(0, 3)

    @pl.loop(0, TR // BS)
    def _(i):
        g, h = i // 2, i % 2
        rows = pl.ds(mult(h * BS, BS), BS)

        def put(pos, value):
            hi, lo = split(value * STEP_TIME)
            cols = pl.ds(mult(pos * BS, BS), BS)
            hrow[0, g, rows, cols] = hi
            hrow[1, g, rows, cols] = lo

        for d in range(-KB, KB + 1):
            u = ext[pl.ds(mult((i + KB + min(d, 0)) * BS, BS), BS), abs(d) * BS : (abs(d) + 1) * BS]
            value = u if d > 0 else u.T if d < 0 else 0.5 * (u + u.T)
            put(h + d + KB, value)
        put((1 - h) * (2 * KB + 1), jnp.zeros((BS, BS), F32))

    @pl.loop(0, TC // BS)
    def _(i):
        j, h = i // 2, i % 2
        cols = pl.ds(mult(h * BS, BS), BS)

        def put(pos, value):
            hi, lo = split(value * -STEP_TIME)
            rows = pl.ds(mult(pos * BS, BS), BS)
            ncol[0, j, rows, cols] = hi
            ncol[1, j, rows, cols] = lo

        for d in range(-KB, KB + 1):
            u = band[pl.ds(mult((i + KB + min(d, 0)) * BS, BS), BS), abs(d) * BS : (abs(d) + 1) * BS]
            value = u if d < 0 else u.T if d > 0 else 0.5 * (u + u.T)
            put(h + d + KB, value)
        put((1 - h) * (2 * KB + 1), jnp.zeros((BS, BS), F32))

    def take_cols(s, slot, g):
        rows = pl.ds(mult(g * W), W)
        for n in range(2):
            col_copy(s, slot, n, g).wait_recv()
        for n in range(2):
            hi, lo = split(colbuf[s, slot, n, rows, :])
            xs[s, n, 0, pl.ds(mult(W + g * W), W), pl.ds(col_dst[slot], W)] = hi
            xs[s, n, 1, pl.ds(mult(W + g * W), W), pl.ds(col_dst[slot], W)] = lo

    def take_rows(s, slot):
        if slot == 0:
            for n in range(2):
                row_copy(s, n).wait_recv()
        else:
            for i in range(4):
                b_direct(s, i).wait_recv()
        for n in range(2):
            hi, lo = split(rowbuf[s, slot, n])
            xs[s, n, 0, pl.ds(row_dst[slot], W), W : W + TC] = hi
            xs[s, n, 1, pl.ds(row_dst[slot], W), W : W + TC] = lo

    def product(s, n, g, j):
        r0, c0 = mult(g * W), mult(j * W)
        hi, lo = xs.at[s, 1 - n, 0], xs.at[s, 1 - n, 1]
        row_h = hi[pl.ds(r0, 3 * W), pl.ds(mult(c0 + W), W)]
        row_l = lo[pl.ds(r0, 3 * W), pl.ds(mult(c0 + W), W)]
        col_h = hi[pl.ds(mult(r0 + W), W), pl.ds(c0, 3 * W)]
        col_l = lo[pl.ds(mult(r0 + W), W), pl.ds(c0, 3 * W)]
        h_h, h_l = hrow[0, g], hrow[1, g]
        n_h, n_l = ncol[0, j], ncol[1, j]
        lhs = jnp.concatenate([h_h, h_h, h_l, col_h, col_l, col_h], axis=1)
        rhs = jnp.concatenate([row_h, row_l, row_h, n_h, n_h, n_l], axis=0)
        total = jnp.dot(lhs, rhs, preferred_element_type=F32)
        return jnp.where(n == 0, 1.0, -1.0).astype(F32) * total

    def last_part(n):
        g = NG - 1 - g_a
        for i in (2 * n, 2 * n + 1):
            b_direct(1, i).wait_recv()
        hi, lo = split(rowbuf[1, 1, n])
        cols = pl.ds(mult(jnp.where(even, 0, 2 * W)), W)
        h_h, h_l = hrow[0, g, :, cols], hrow[1, g, :, cols]
        lhs = jnp.concatenate([h_h, h_h, h_l], axis=1)
        rhs = jnp.concatenate([hi, lo, hi], axis=0)
        rows = pl.ds(mult(g * W), W)
        dens[1 - n, rows, :] += (-0.5 if n == 0 else 0.5) * jnp.dot(lhs, rhs, preferred_element_type=F32)

    for s in range(2):

        @pl.loop(0, NG)
        def _(t):
            g = order(s, t)
            take_cols(s, 0, g)

            @pl.when(has_y)
            def _():
                take_cols(s, 1, g)

            @pl.when(t == 2 * s)
            def _():
                take_rows(s, 0)

            if s == 0:

                @pl.when((t == 3) & has_b)
                def _():
                    take_rows(s, 1)

            @pl.loop(0, 2 * NJ)
            def _(i):
                n, j = i // NJ, i % NJ
                value = product(s, n, g, j)
                rows, cols = pl.ds(mult(g * W), W), pl.ds(mult(j * W), W)
                if s == 0:
                    grad[n, rows, cols] = value
                    hi, lo = split(value)
                    xs[1, n, 0, pl.ds(mult(W + g * W), W), pl.ds(mult(W + j * W), W)] = hi
                    xs[1, n, 1, pl.ds(mult(W + g * W), W), pl.ds(mult(W + j * W), W)] = lo
                else:
                    dens[n, rows, cols] = dens[n, rows, cols] + grad[n, rows, cols] + 0.5 * value

            if s == 0:

                @pl.when(t == 0)
                def _():
                    for n in range(2):
                        row_copy(1, n).start()

                start_cols(1, t)

                @pl.when(t == 3)
                def _():
                    b_far(1)
                    pass_on(1, 1)
                    b_near(1)
                    b_pass(1)
                    pass_on(1, 3)

    @pl.when(has_b)
    def _():
        for n in range(2):
            last_part(n)

    for s in range(2):
        for n in range(2):
            row_copy(s, n).wait_send()

        @pl.when(has_b)
        def _():
            for i in range(4):
                b_direct(s, i).wait_send()

        for i in range(1, 4):

            @pl.when(i > depth)
            def _():
                b_second(s, i).wait_send()

        @pl.loop(0, NG)
        def _(g):
            for n in range(2):
                col_copy(s, 0, n, g).wait_send()

            @pl.when(has_y)
            def _():
                for n in range(2):
                    col_copy(s, 1, n, g).wait_send()

    @pl.when(is_relay)
    def _():
        for s in range(2):
            for n in range(2):
                relay_copy(s, n).wait_send()

    @pl.when(last)
    def _():
        for q in LATE:
            above_copy(q).wait_send()

    for q in range(6):

        @pl.when(goes_across(q))
        def _():
            across_copy(q).wait_send()

        @pl.when(goes_along(q))
        def _():
            along_copy(q).wait_send()


def shards(dens_real, dens_imag, upper_band, pattern):
    dma = pltpu.SemaphoreType.DMA
    anywhere = pl.BlockSpec(memory_space=pl.ANY)
    out = pl.pallas_call(
        kernel,
        out_shape=pltpu.VMEM((2, TR, TC), F32),
        in_specs=[anywhere] * 3 + [pl.BlockSpec(memory_space=pltpu.SMEM)],
        out_specs=pl.BlockSpec(memory_space=pltpu.VMEM),
        scratch_shapes=[
            pltpu.VMEM((2, TR, TC), F32),
            pltpu.VMEM((2, 2, 2, TR + 2 * W, TC + 2 * W), BF16),
            pltpu.VMEM((2, 2, 2, W, TC), F32),
            pltpu.VMEM((2, 2, 2, TR, W), F32),
            pltpu.VMEM((TR + W, 3 * BS), F32),
            pltpu.VMEM((TC + W, 3 * BS), F32),
            pltpu.VMEM((2, NG, W, 3 * W), BF16),
            pltpu.VMEM((2, NJ, 3 * W, W), BF16),
            pltpu.VMEM((2, 2, W, W), F32),
            pltpu.VMEM((2, 4, BS, TC), F32),
            dma((9,)),
            dma((2, 2)),
            dma((2, 2)),
            dma((2, 4)),
            dma((2, 4)),
            dma((2, 4)),
            dma((2, 4)),
            dma((2, 2, 2, NG)),
            dma((2, 2, 2, NG)),
            dma((2,)),
            dma((2,)),
            dma((6,)),
            dma((6,)),
            dma((6,)),
            dma((2, 2)),
            dma((2, 2)),
        ],
        compiler_params=pltpu.CompilerParams(collective_id=0, has_side_effects=True, vmem_limit_bytes=55 << 20),
        name="heun",
    )(dens_real, dens_imag, upper_band, pattern)
    return out[0], out[1]


def solution(mesh):
    in_specs = (P("row", "col"), P("row", "col"), P("row", None), P("row", None))
    out_specs = (P("row", "col"), P("row", "col"))
    return jax.shard_map(shards, mesh=mesh, in_specs=in_specs, out_specs=out_specs, check_vma=False)
```

```python
import jax
import jax.numpy as jnp
from jax import lax
from jax.experimental import pallas as pl
from jax.experimental.pallas import tpu as pltpu
from jax.sharding import PartitionSpec as P

BS = 128
KB = 2
NB = 64
STEP_TIME = 0.3
MESH = pl.DeviceIdType.MESH
F32 = jnp.float32
BF16 = jnp.bfloat16
TR = 1024
TC = 512
W = KB * BS
NG = TR // W
NJ = TC // W
ROWS = 8
COLS = 16
PIECES = [(0, BS, 2 * BS, BS), (BS, BS, BS, 2 * BS)] + [(q * BS, BS, 0, 3 * BS) for q in range(2, 6)]
LATE = (0, 1)
EARLY = (2, 3, 4, 5)


def mult(x, n=W):
    return pl.multiple_of(x, n)


def split(x):
    hi = x.astype(BF16)
    return hi, (x - hi.astype(F32)).astype(BF16)


def kernel(a_ref, b_ref, u_ref, pat_ref, dens, grad, xs, rowbuf, colbuf, ext, band, hrow, ncol, relay, zrelay,
           lsem, rs_s, rs_r, bs_s, bs_r, bz_s, bz_r, cs_s, cs_r, ab_s, ab_r, sw_s, bk_s, al_s, cr_s, bd_r, rl_s, rl_r):
    r, c = lax.axis_index("row"), lax.axis_index("col")
    even, core = r % 2 == 0, c % 2
    k = c // 2
    z, zk, half = r // 2, k // 2, r % 2
    step_up = k % 2 == 0
    dist = jnp.where(step_up, z - zk, zk - z)
    dist = (dist + 4) % 4
    is_src = r == k
    near = half == k % 2
    a_row = jnp.where(even, r + 1, r - 1)
    b_row = jnp.where(even, r - 1, r + 1)
    has_b = (b_row >= 0) & (b_row < ROWS)
    cc_col = jnp.where(core == 0, c + 1, c - 1)
    cy_col = jnp.where(core == 0, c - 1, c + 1)
    has_y = (cy_col >= 0) & (cy_col < COLS)
    hub = (c == 7) | (c == 8)
    mine = jnp.minimum(c, COLS - 1 - c)
    is_relay = mine < 6
    relay_n = mine % 2
    relay_turn = jnp.where(mine < 2, 1, jnp.where(mine < 4, 3, 2))
    relay_to = jnp.where(c < 8, 8, 7)
    z_up, z_dn = (r + 2) % ROWS, (r + 6) % ROWS
    z_next, z_back = jnp.where(step_up, z_up, z_dn), jnp.where(step_up, z_dn, z_up)
    depth = jnp.where(even, z, 3 - z)
    first_far = depth
    z_relay = jnp.where(even, z_dn, z_up)
    first = r > 0
    last = r < ROWS - 1

    row_dev = ((a_row, c), (b_row, c))
    row_src = (mult(jnp.where(even, TR - W, 0)), mult(jnp.where(even, 0, TR - W)))
    row_dst = (mult(jnp.where(even, TR + W, 0)), mult(jnp.where(even, 0, TR + W)))
    col_dev = ((r, cc_col), (r, cy_col))
    col_src = (mult(jnp.where(core == 0, TC - W, 0)), mult(jnp.where(core == 0, 0, TC - W)))
    col_dst = (mult(jnp.where(core == 0, TC + W, 0)), mult(jnp.where(core == 0, 0, TC + W)))
    g_a = jnp.where(even, NG - 1, 0)
    ext_off = mult(core * TC, BS)

    def order(s, t):
        if s == 0:
            return jnp.where(t == 0, g_a, jnp.where(t == 3, NG - 1 - g_a, t))
        return jnp.where(t < 2, t + 1, jnp.where(t == 2, g_a, NG - 1 - g_a))

    def remote(src, dst, ss, rs, dev):
        return pltpu.make_async_remote_copy(src, dst, ss, rs, device_id=dev, device_id_type=MESH)

    def row_copy(s, n):
        src = (a_ref, b_ref)[n] if s == 0 else grad.at[n]
        return remote(src.at[pl.ds(row_src[0], W), :], rowbuf.at[s, 0, n], rs_s.at[s, n], rs_r.at[s, n], row_dev[0])

    def b_src(s, i):
        src = (a_ref, b_ref)[i // 2] if s == 0 else grad.at[i // 2]
        return src.at[pl.ds(mult(row_src[1] + i % 2 * BS, BS), BS), :]

    def b_dst(s, i):
        return rowbuf.at[s, 1, i // 2, i % 2 * BS : (i % 2 + 1) * BS, :]

    def b_direct(s, i):
        return remote(b_src(s, i), b_dst(s, i), bs_s.at[s, i], bs_r.at[s, i], row_dev[1])

    def b_first(s, i):
        return remote(b_src(s, i), zrelay.at[s, i], bs_s.at[s, i], bz_r.at[s, i], (z_relay, c))

    def b_second(s, i):
        return remote(zrelay.at[s, i], b_dst(s, i), bz_s.at[s, i], bs_r.at[s, i], (a_row, c))

    def b_far(s):
        for i in range(4):

            @pl.when(has_b & (i >= first_far))
            def _():
                b_first(s, i).start()

    def b_near(s, pieces=(0, 1, 2)):
        for i in pieces:

            @pl.when(has_b & (i < first_far))
            def _():
                b_direct(s, i).start()

    def b_pass(s):
        for i in range(1, 4):

            @pl.when(i > depth)
            def _():
                b_first(s, i).wait_recv()
                b_second(s, i).start()

    def col_copy(s, slot, n, g):
        src = (a_ref, b_ref)[n] if s == 0 else grad.at[n]
        rows = pl.ds(mult(g * W), W)
        return remote(src.at[rows, pl.ds(col_src[slot], W)], colbuf.at[s, slot, n, rows, :], cs_s.at[s, slot, n, g], cs_r.at[s, slot, n, g], col_dev[slot])

    def hub_copy(s, n, t):
        g = order(0, t)
        src = (a_ref, b_ref)[n] if s == 0 else grad.at[n]
        turn = t if s == 0 else jnp.where(t == 0, 3, t)
        near_col = jnp.where(turn == 1, 0, jnp.where(turn == 2, 4, 2)) + n
        to = jnp.where(c < 8, near_col, COLS - 1 - near_col)
        return remote(src.at[pl.ds(mult(g * W), W), pl.ds(col_src[1], W)], relay.at[s], cs_s.at[s, 1, n, g], rl_r.at[s], (r, to))

    def relay_copy(s):
        g = order(0, relay_turn if s == 0 else relay_turn % 3)
        return remote(relay.at[s], colbuf.at[s, 1, relay_n, pl.ds(mult(g * W), W), :], rl_s.at[s], cs_r.at[s, 1, relay_n, g], (r, relay_to))

    def pass_on(s, which):
        @pl.when(is_relay & which)
        def _():
            hub_copy(s, 0, 1).wait_recv()
            relay_copy(s).start()

    def above_copy(q):
        r0, nr, c0, nc = PIECES[q]
        return remote(ext.at[TR + r0 : TR + r0 + nr, c0 : c0 + nc], ext.at[r0 : r0 + nr, c0 : c0 + nc], ab_s.at[q], ab_r.at[q], (jnp.minimum(r + 1, ROWS - 1), c))

    def swap_copy(q):
        return remote(piece(ext, q), piece(ext, q), sw_s.at[q], ab_r.at[q], (r, cc_col))

    def take_above():
        for q in LATE:

            @pl.when(core == q)
            def _():
                above_copy(q).wait_recv()
                swap_copy(q).start()
                above_copy(1 - q).wait_recv()


    def piece(ref, q, off=0):
        if isinstance(q, int) and q in LATE:
            r0, nr, c0, nc = PIECES[q]
            return ref.at[pl.ds(mult(off + r0, BS), nr), c0 : c0 + nc]
        return ref.at[pl.ds(mult(off + q * BS, BS), BS), :]

    def part(q):
        return 0 if isinstance(q, int) and q in LATE else q - 2

    def hops(q):
        return (dist - part(q) + 4) % 4

    def goes_along(q):
        return jnp.where(near, dist + 1, hops(q)) < 3

    def goes_across(q):
        return near & (dist == part(q))

    def along_copy(q):
        return remote(piece(band, q), piece(band, q), al_s.at[q], bd_r.at[q], (z_next, c))

    def across_copy(q):
        return remote(piece(band, q), piece(band, q), cr_s.at[q], bd_r.at[q], (a_row, c))

    def back_copy(q):
        return remote(piece(band, q), piece(band, q), bk_s.at[q], bd_r.at[q], (z_back, c))

    def along(q):
        @pl.when(is_src)
        def _():
            back_copy(q).start()

        @pl.when(goes_along(q))
        def _():
            along_copy(q).start()

    def forward(q):
        @pl.when(goes_across(q))
        def _():
            across_copy(q).start()

        along(q)

    def own_piece(q):
        return pltpu.make_async_copy(piece(ext, q, ext_off), piece(band, q), lsem.at[3 + q])

    barrier = pltpu.get_barrier_semaphore()

    def greet(dev):
        pl.semaphore_signal(barrier, inc=1, device_id=dev, device_id_type=MESH)

    for dev in (row_dev[0], col_dev[0], (z_up, c), (z_dn, c)):
        greet(dev)

    @pl.when(has_b)
    def _():
        greet(row_dev[1])

    @pl.when(has_y)
    def _():
        greet(col_dev[1])

    loads = [
        pltpu.make_async_copy(a_ref, dens.at[0], lsem.at[0]),
        pltpu.make_async_copy(b_ref, dens.at[1], lsem.at[1]),
        pltpu.make_async_copy(u_ref, ext.at[W:, :], lsem.at[2]),
    ]

    for cp in loads[::-1]:
        cp.start()

    @pl.when(jnp.logical_not(first))
    def _():
        ext[0:W, :] = jnp.zeros((W, 3 * BS), F32)

    loads[2].wait()

    @pl.loop(0, TR // BS)
    def _(i):
        rows = pl.ds(mult(W + i * BS, BS), BS)
        for d in range(1, KB + 1):
            present = (pat_ref[i, d - 1] > 0) & (r * (TR // BS) + i + d < NB)
            cols = slice(d * BS, (d + 1) * BS)
            ext[rows, cols] = ext[rows, cols] * jnp.where(present, 1.0, 0.0).astype(F32)

    @pl.when(is_src)
    def _():
        for q in EARLY:
            own_piece(q).start()

    @pl.when(hub)
    def _():
        for col in (*range(6), *range(10, COLS)):
            greet((r, col))

    @pl.when(is_relay)
    def _():
        for col in (7, 8):
            greet((r, col))

    pl.semaphore_wait(barrier, 4 + has_b.astype(jnp.int32) + has_y.astype(jnp.int32) + jnp.where(hub, 12, 0) + jnp.where(is_relay, 2, 0))

    for q in LATE:

        @pl.when(last & (core == q))
        def _():
            above_copy(q).start()

    def start_b():
        pass_on(0, relay_turn < 3)
        b_near(0)
        b_pass(0)

    @pl.when(is_src)
    def _():
        own_piece(2).wait()
        across_copy(2).start()

    def hub_direct():
        @pl.when(hub)
        def _():
            for n in range(2):
                col_copy(0, 1, n, g_a).start()

    row_copy(0, 0).start()

    @pl.when(jnp.logical_not(near))
    def _():
        hub_direct()
        row_copy(0, 1).start()

    @pl.when(is_src)
    def _():
        for q in (5, 4, 3):
            own_piece(q).wait()
            along(q)
        along(2)

    b_far(0)

    def start_cols(s, t):
        g = order(0, t)
        for n in range(2):
            col_copy(s, 0, n, g).start()

        @pl.when(has_y & (jnp.logical_not(hub) | ((t == 3) & (s == 1))))
        def _():
            for n in range(2):
                col_copy(s, 1, n, g).start()

        @pl.when(hub & (t > 0 if s == 0 else t < 3))
        def _():
            for n in range(2):
                hub_copy(s, n, t).start()

    @pl.loop(0, NG)
    def _(t):
        start_cols(0, t)

    def clear_rows(s):
        for n in range(2):
            for p in range(2):
                xs[s, n, p, pl.ds(row_dst[1], W), W : W + TC] = jnp.zeros((W, TC), BF16)

    @pl.when(jnp.logical_not(has_b))
    def _():
        clear_rows(0)

    clear_rows(1)

    @pl.when(jnp.logical_not(has_y))
    def _():
        for s in range(2):
            for n in range(2):
                for p in range(2):
                    xs[s, n, p, :, pl.ds(col_dst[1], W)] = jnp.zeros((TR + 2 * W, W), BF16)

    loads[0].wait()
    loads[1].wait()

    @pl.loop(0, 2 * NG)
    def _(i):
        n, g = i // NG, i % NG
        hi, lo = split(dens[n, pl.ds(mult(g * W), W), :])
        xs[0, n, 0, pl.ds(mult(W + g * W), W), W : W + TC] = hi
        xs[0, n, 1, pl.ds(mult(W + g * W), W), W : W + TC] = lo

    @pl.when(is_src)
    def _():
        @pl.when(first)
        def _():
            take_above()

        for q in LATE:
            own_piece(q).start()
        for q in LATE:
            own_piece(q).wait()
            forward(q)
        row_copy(0, 1).start()
        hub_direct()
        start_b()

    @pl.when(jnp.logical_not(is_src))
    def _():
        for e in range(4):
            q = 2 + jnp.where(near, 3 - e, (dist - e + 4) % 4)
            along_copy(q).wait_recv()
            forward(q)

            @pl.when(goes_across(q))
            def _():
                row_copy(0, 1).start()
                hub_direct()

            @pl.when(e == jnp.where(near, 2, 0))
            def _():
                start_b()

            @pl.when(e == jnp.where(near, 3, jnp.minimum(dist + 1, 3)))
            def _():
                for p in LATE:
                    along_copy(p).wait_recv()
                    forward(p)

        @pl.when(first)
        def _():
            take_above()

    pass_on(0, relay_turn == 3)

    @pl.loop(0, TR // BS)
    def _(i):
        g, h = i // 2, i % 2
        rows = pl.ds(mult(h * BS, BS), BS)

        def put(pos, value):
            hi, lo = split(value * STEP_TIME)
            cols = pl.ds(mult(pos * BS, BS), BS)
            hrow[0, g, rows, cols] = hi
            hrow[1, g, rows, cols] = lo

        for d in range(-KB, KB + 1):
            u = ext[pl.ds(mult((i + KB + min(d, 0)) * BS, BS), BS), abs(d) * BS : (abs(d) + 1) * BS]
            value = u if d > 0 else u.T if d < 0 else 0.5 * (u + u.T)
            put(h + d + KB, value)
        put((1 - h) * (2 * KB + 1), jnp.zeros((BS, BS), F32))

    @pl.loop(0, TC // BS)
    def _(i):
        j, h = i // 2, i % 2
        cols = pl.ds(mult(h * BS, BS), BS)

        def put(pos, value):
            hi, lo = split(value * -STEP_TIME)
            rows = pl.ds(mult(pos * BS, BS), BS)
            ncol[0, j, rows, cols] = hi
            ncol[1, j, rows, cols] = lo

        for d in range(-KB, KB + 1):
            u = band[pl.ds(mult((i + KB + min(d, 0)) * BS, BS), BS), abs(d) * BS : (abs(d) + 1) * BS]
            value = u if d < 0 else u.T if d > 0 else 0.5 * (u + u.T)
            put(h + d + KB, value)
        put((1 - h) * (2 * KB + 1), jnp.zeros((BS, BS), F32))

    def take_cols(s, slot, g):
        rows = pl.ds(mult(g * W), W)
        for n in range(2):
            col_copy(s, slot, n, g).wait_recv()
        for n in range(2):
            hi, lo = split(colbuf[s, slot, n, rows, :])
            xs[s, n, 0, pl.ds(mult(W + g * W), W), pl.ds(col_dst[slot], W)] = hi
            xs[s, n, 1, pl.ds(mult(W + g * W), W), pl.ds(col_dst[slot], W)] = lo

    def take_rows(s, slot):
        if slot == 0:
            for n in range(2):
                row_copy(s, n).wait_recv()
        else:
            for i in range(4):
                b_direct(s, i).wait_recv()
        for n in range(2):
            hi, lo = split(rowbuf[s, slot, n])
            xs[s, n, 0, pl.ds(row_dst[slot], W), W : W + TC] = hi
            xs[s, n, 1, pl.ds(row_dst[slot], W), W : W + TC] = lo

    def product(s, n, g, j):
        r0, c0 = mult(g * W), mult(j * W)
        hi, lo = xs.at[s, 1 - n, 0], xs.at[s, 1 - n, 1]
        row_h = hi[pl.ds(r0, 3 * W), pl.ds(mult(c0 + W), W)]
        row_l = lo[pl.ds(r0, 3 * W), pl.ds(mult(c0 + W), W)]
        col_h = hi[pl.ds(mult(r0 + W), W), pl.ds(c0, 3 * W)]
        col_l = lo[pl.ds(mult(r0 + W), W), pl.ds(c0, 3 * W)]
        h_h, h_l = hrow[0, g], hrow[1, g]
        n_h, n_l = ncol[0, j], ncol[1, j]
        lhs = jnp.concatenate([h_h, h_h, h_l, col_h, col_l, col_h], axis=1)
        rhs = jnp.concatenate([row_h, row_l, row_h, n_h, n_h, n_l], axis=0)
        total = jnp.dot(lhs, rhs, preferred_element_type=F32)
        return jnp.where(n == 0, 1.0, -1.0).astype(F32) * total

    def last_part(n):
        g = NG - 1 - g_a
        for i in (2 * n, 2 * n + 1):
            b_direct(1, i).wait_recv()
        hi, lo = split(rowbuf[1, 1, n])
        cols = pl.ds(mult(jnp.where(even, 0, 2 * W)), W)
        h_h, h_l = hrow[0, g, :, cols], hrow[1, g, :, cols]
        lhs = jnp.concatenate([h_h, h_h, h_l], axis=1)
        rhs = jnp.concatenate([hi, lo, hi], axis=0)
        rows = pl.ds(mult(g * W), W)
        dens[1 - n, rows, :] += (-0.5 if n == 0 else 0.5) * jnp.dot(lhs, rhs, preferred_element_type=F32)

    for s in range(2):

        @pl.loop(0, NG)
        def _(t):
            g = order(s, t)
            take_cols(s, 0, g)

            @pl.when(has_y)
            def _():
                take_cols(s, 1, g)

            @pl.when(t == 2 * s)
            def _():
                take_rows(s, 0)

            if s == 0:

                @pl.when((t == 3) & has_b)
                def _():
                    take_rows(s, 1)

            @pl.loop(0, 2 * NJ)
            def _(i):
                n, j = i // NJ, i % NJ
                value = product(s, n, g, j)
                rows, cols = pl.ds(mult(g * W), W), pl.ds(mult(j * W), W)
                if s == 0:
                    grad[n, rows, cols] = value
                    hi, lo = split(value)
                    xs[1, n, 0, pl.ds(mult(W + g * W), W), pl.ds(mult(W + j * W), W)] = hi
                    xs[1, n, 1, pl.ds(mult(W + g * W), W), pl.ds(mult(W + j * W), W)] = lo
                else:
                    dens[n, rows, cols] = dens[n, rows, cols] + grad[n, rows, cols] + 0.5 * value

            if s == 0:

                @pl.when(t == 0)
                def _():
                    for n in range(2):
                        row_copy(1, n).start()

                start_cols(1, t)

                @pl.when(t == 3)
                def _():
                    b_far(1)
                    pass_on(1, relay_turn != 2)
                    b_near(1, (0,))
                    pass_on(1, relay_turn == 2)
                    b_near(1, (1, 2))
                    b_pass(1)

    @pl.when(has_b)
    def _():
        for n in range(2):
            last_part(n)

    for s in range(2):
        for n in range(2):
            row_copy(s, n).wait_send()

        @pl.when(has_b)
        def _():
            for i in range(4):
                b_direct(s, i).wait_send()

        for i in range(1, 4):

            @pl.when(i > depth)
            def _():
                b_second(s, i).wait_send()

        @pl.loop(0, NG)
        def _(g):
            for n in range(2):
                col_copy(s, 0, n, g).wait_send()

            @pl.when(has_y)
            def _():
                for n in range(2):
                    col_copy(s, 1, n, g).wait_send()

    @pl.when(is_relay)
    def _():
        for s in range(2):
            relay_copy(s).wait_send()

    for q in LATE:

        @pl.when(last & (core == q))
        def _():
            above_copy(q).wait_send()

        @pl.when(first & (core == q))
        def _():
            swap_copy(q).wait_send()

    for q in range(6):

        @pl.when(goes_across(q))
        def _():
            across_copy(q).wait_send()

        @pl.when(is_src)
        def _():
            back_copy(q).wait_send()

        @pl.when(goes_along(q))
        def _():
            along_copy(q).wait_send()


def shards(dens_real, dens_imag, upper_band, pattern):
    dma = pltpu.SemaphoreType.DMA
    anywhere = pl.BlockSpec(memory_space=pl.ANY)
    out = pl.pallas_call(
        kernel,
        out_shape=pltpu.VMEM((2, TR, TC), F32),
        in_specs=[anywhere] * 3 + [pl.BlockSpec(memory_space=pltpu.SMEM)],
        out_specs=pl.BlockSpec(memory_space=pltpu.VMEM),
        scratch_shapes=[
            pltpu.VMEM((2, TR, TC), F32),
            pltpu.VMEM((2, 2, 2, TR + 2 * W, TC + 2 * W), BF16),
            pltpu.VMEM((2, 2, 2, W, TC), F32),
            pltpu.VMEM((2, 2, 2, TR, W), F32),
            pltpu.VMEM((TR + W, 3 * BS), F32),
            pltpu.VMEM((TC + W, 3 * BS), F32),
            pltpu.VMEM((2, NG, W, 3 * W), BF16),
            pltpu.VMEM((2, NJ, 3 * W, W), BF16),
            pltpu.VMEM((2, W, W), F32),
            pltpu.VMEM((2, 4, BS, TC), F32),
            dma((9,)),
            dma((2, 2)),
            dma((2, 2)),
            dma((2, 4)),
            dma((2, 4)),
            dma((2, 4)),
            dma((2, 4)),
            dma((2, 2, 2, NG)),
            dma((2, 2, 2, NG)),
            dma((2,)),
            dma((2,)),
            dma((2,)),
            dma((6,)),
            dma((6,)),
            dma((6,)),
            dma((6,)),
            dma((2,)),
            dma((2,)),
        ],
        compiler_params=pltpu.CompilerParams(collective_id=0, has_side_effects=True, vmem_limit_bytes=55 << 20),
        name="heun",
    )(dens_real, dens_imag, upper_band, pattern)
    return out[0], out[1]


def solution(mesh):
    in_specs = (P("row", "col"), P("row", "col"), P("row", None), P("row", None))
    out_specs = (P("row", "col"), P("row", "col"))
    return jax.shard_map(shards, mesh=mesh, in_specs=in_specs, out_specs=out_specs, check_vma=False)
```

```python
import jax
import jax.numpy as jnp
from jax import lax
from jax.experimental import pallas as pl
from jax.experimental.pallas import tpu as pltpu
from jax.sharding import PartitionSpec as P

BS = 128
KB = 2
NB = 64
STEP_TIME = 0.3
MESH = pl.DeviceIdType.MESH
F32 = jnp.float32
BF16 = jnp.bfloat16
TR = 1024
TC = 512
W = KB * BS
NG = TR // W
NJ = TC // W
ROWS = 8
COLS = 16
PIECES = [(0, BS, 2 * BS, BS), (BS, BS, BS, 2 * BS)] + [(q * BS, BS, 0, 3 * BS) for q in range(2, 6)]
LATE = (0, 1)
EARLY = (2, 3, 4, 5)


def mult(x, n=W):
    return pl.multiple_of(x, n)


def split(x):
    hi = x.astype(BF16)
    return hi, (x - hi.astype(F32)).astype(BF16)


def kernel(a_ref, b_ref, u_ref, pat_ref, dens, grad, xs, rowbuf, colbuf, ext, band, hrow, ncol, relay, zrelay,
           lsem, rs_s, rs_r, bs_s, bs_r, bz_s, bz_r, cs_s, cs_r, ab_s, ab_r, sw_s, mt_s, bk_s, al_s, cr_s, bd_r, rl_s, rl_r):
    r, c = lax.axis_index("row"), lax.axis_index("col")
    even, core = r % 2 == 0, c % 2
    k = c // 2
    z, zk, half = r // 2, k // 2, r % 2
    step_up = k % 2 == 0
    dist = jnp.where(step_up, z - zk, zk - z)
    dist = (dist + 4) % 4
    is_src = r == k
    near = half == k % 2
    a_row = jnp.where(even, r + 1, r - 1)
    b_row = jnp.where(even, r - 1, r + 1)
    has_b = (b_row >= 0) & (b_row < ROWS)
    cc_col = jnp.where(core == 0, c + 1, c - 1)
    cy_col = jnp.where(core == 0, c - 1, c + 1)
    has_y = (cy_col >= 0) & (cy_col < COLS)
    hub = (c == 7) | (c == 8)
    mine = jnp.minimum(c, COLS - 1 - c)
    is_relay = mine < 6
    relay_n = mine % 2
    relay_turn = jnp.where(mine < 2, 1, jnp.where(mine < 4, 3, 2))
    relay_to = jnp.where(c < 8, 8, 7)
    z_up, z_dn = (r + 2) % ROWS, (r + 6) % ROWS
    z_next, z_back = jnp.where(step_up, z_up, z_dn), jnp.where(step_up, z_dn, z_up)
    depth = jnp.where(even, z, 3 - z)
    first_far = depth
    z_relay = jnp.where(even, z_dn, z_up)
    first = r > 0
    last = r < ROWS - 1

    row_dev = ((a_row, c), (b_row, c))
    row_src = (mult(jnp.where(even, TR - W, 0)), mult(jnp.where(even, 0, TR - W)))
    row_dst = (mult(jnp.where(even, TR + W, 0)), mult(jnp.where(even, 0, TR + W)))
    col_dev = ((r, cc_col), (r, cy_col))
    col_src = (mult(jnp.where(core == 0, TC - W, 0)), mult(jnp.where(core == 0, 0, TC - W)))
    col_dst = (mult(jnp.where(core == 0, TC + W, 0)), mult(jnp.where(core == 0, 0, TC + W)))
    g_a = jnp.where(even, NG - 1, 0)
    ext_off = mult(core * TC, BS)

    def order(s, t):
        if s == 0:
            return jnp.where(t == 0, g_a, jnp.where(t == 3, NG - 1 - g_a, t))
        return jnp.where(t < 2, t + 1, jnp.where(t == 2, g_a, NG - 1 - g_a))

    def remote(src, dst, ss, rs, dev):
        return pltpu.make_async_remote_copy(src, dst, ss, rs, device_id=dev, device_id_type=MESH)

    def row_copy(s, n):
        src = (a_ref, b_ref)[n] if s == 0 else grad.at[n]
        return remote(src.at[pl.ds(row_src[0], W), :], rowbuf.at[s, 0, n], rs_s.at[s, n], rs_r.at[s, n], row_dev[0])

    def b_src(s, i):
        src = (a_ref, b_ref)[i // 2] if s == 0 else grad.at[i // 2]
        return src.at[pl.ds(mult(row_src[1] + i % 2 * BS, BS), BS), :]

    def b_dst(s, i):
        return rowbuf.at[s, 1, i // 2, i % 2 * BS : (i % 2 + 1) * BS, :]

    def b_direct(s, i):
        return remote(b_src(s, i), b_dst(s, i), bs_s.at[s, i], bs_r.at[s, i], row_dev[1])

    def b_first(s, i):
        return remote(b_src(s, i), zrelay.at[s, i], bs_s.at[s, i], bz_r.at[s, i], (z_relay, c))

    def b_second(s, i):
        return remote(zrelay.at[s, i], b_dst(s, i), bz_s.at[s, i], bs_r.at[s, i], (a_row, c))

    def b_far(s):
        for i in range(4):

            @pl.when(has_b & (i >= first_far))
            def _():
                b_first(s, i).start()

    def b_near(s, pieces=(0, 1, 2)):
        for i in pieces:

            @pl.when(has_b & (i < first_far))
            def _():
                b_direct(s, i).start()

    def b_pass(s):
        for i in range(1, 4):

            @pl.when(i > depth)
            def _():
                b_first(s, i).wait_recv()
                b_second(s, i).start()

    def col_copy(s, slot, n, g):
        src = (a_ref, b_ref)[n] if s == 0 else grad.at[n]
        rows = pl.ds(mult(g * W), W)
        return remote(src.at[rows, pl.ds(col_src[slot], W)], colbuf.at[s, slot, n, rows, :], cs_s.at[s, slot, n, g], cs_r.at[s, slot, n, g], col_dev[slot])

    def hub_copy(s, n, t):
        g = order(0, t)
        src = (a_ref, b_ref)[n] if s == 0 else grad.at[n]
        turn = t if s == 0 else jnp.where(t == 0, 3, t)
        near_col = jnp.where(turn == 1, 0, jnp.where(turn == 2, 4, 2)) + n
        to = jnp.where(c < 8, near_col, COLS - 1 - near_col)
        return remote(src.at[pl.ds(mult(g * W), W), pl.ds(col_src[1], W)], relay.at[s], cs_s.at[s, 1, n, g], rl_r.at[s], (r, to))

    def relay_copy(s):
        g = order(0, relay_turn if s == 0 else relay_turn % 3)
        return remote(relay.at[s], colbuf.at[s, 1, relay_n, pl.ds(mult(g * W), W), :], rl_s.at[s], cs_r.at[s, 1, relay_n, g], (r, relay_to))

    def pass_on(s, which):
        @pl.when(is_relay & which)
        def _():
            hub_copy(s, 0, 1).wait_recv()
            relay_copy(s).start()

    def above_copy(q):
        r0, nr, c0, nc = PIECES[q]
        return remote(ext.at[TR + r0 : TR + r0 + nr, c0 : c0 + nc], ext.at[r0 : r0 + nr, c0 : c0 + nc], ab_s.at[q], ab_r.at[q], (jnp.minimum(r + 1, ROWS - 1), c))

    def swap_copy(q):
        return remote(piece(ext, q), piece(ext, q), sw_s.at[q], ab_r.at[q], (r, cc_col))

    def take_above():
        for q in LATE:

            @pl.when(core == q)
            def _():
                above_copy(q).wait_recv()
                swap_copy(q).start()
                above_copy(1 - q).wait_recv()


    def piece(ref, q, off=0):
        if isinstance(q, int) and q in LATE:
            r0, nr, c0, nc = PIECES[q]
            return ref.at[pl.ds(mult(off + r0, BS), nr), c0 : c0 + nc]
        return ref.at[pl.ds(mult(off + q * BS, BS), BS), :]

    def part(q):
        return 0 if isinstance(q, int) and q in LATE else q - 2

    def hops(q):
        return (dist - part(q) + 4) % 4

    def travels(q):
        return core == 0 if isinstance(q, int) and q in LATE else True

    def goes_along(q):
        return (jnp.where(near, dist + 1, hops(q)) < 3) & travels(q)

    def goes_across(q):
        return near & (dist == part(q)) & travels(q)

    def goes_back(q):
        return is_src & travels(q)

    def mate_copy(p):
        r0, nr, c0, nc = PIECES[p]
        return remote(band.at[r0 + 4 * BS : r0 + 4 * BS + nr, c0 : c0 + nc], piece(band, p), mt_s.at[p], bd_r.at[p], (r, cc_col))

    def along_copy(q):
        return remote(piece(band, q), piece(band, q), al_s.at[q], bd_r.at[q], (z_next, c))

    def across_copy(q):
        return remote(piece(band, q), piece(band, q), cr_s.at[q], bd_r.at[q], (a_row, c))

    def back_copy(q):
        return remote(piece(band, q), piece(band, q), bk_s.at[q], bd_r.at[q], (z_back, c))

    def along(q):
        @pl.when(goes_back(q))
        def _():
            back_copy(q).start()

        @pl.when(goes_along(q))
        def _():
            along_copy(q).start()

    def forward(q):
        @pl.when(goes_across(q))
        def _():
            across_copy(q).start()

        along(q)

    def own_piece(q):
        return pltpu.make_async_copy(piece(ext, q, ext_off), piece(band, q), lsem.at[3 + q])

    barrier = pltpu.get_barrier_semaphore()

    def greet(dev):
        pl.semaphore_signal(barrier, inc=1, device_id=dev, device_id_type=MESH)

    for dev in (row_dev[0], col_dev[0], (z_up, c), (z_dn, c)):
        greet(dev)

    @pl.when(has_b)
    def _():
        greet(row_dev[1])

    @pl.when(has_y)
    def _():
        greet(col_dev[1])

    loads = [
        pltpu.make_async_copy(a_ref, dens.at[0], lsem.at[0]),
        pltpu.make_async_copy(b_ref, dens.at[1], lsem.at[1]),
        pltpu.make_async_copy(u_ref, ext.at[W:, :], lsem.at[2]),
    ]

    for cp in loads[::-1]:
        cp.start()

    @pl.when(jnp.logical_not(first))
    def _():
        ext[0:W, :] = jnp.zeros((W, 3 * BS), F32)

    loads[2].wait()

    @pl.loop(0, TR // BS)
    def _(i):
        rows = pl.ds(mult(W + i * BS, BS), BS)
        for d in range(1, KB + 1):
            present = (pat_ref[d - 1, i] > 0) & (r * (TR // BS) + i + d < NB)
            cols = slice(d * BS, (d + 1) * BS)
            ext[rows, cols] = ext[rows, cols] * jnp.where(present, 1.0, 0.0).astype(F32)

    @pl.when(is_src)
    def _():
        for q in EARLY:
            own_piece(q).start()

    @pl.when(hub)
    def _():
        for col in (*range(6), *range(10, COLS)):
            greet((r, col))

    @pl.when(is_relay)
    def _():
        for col in (7, 8):
            greet((r, col))

    pl.semaphore_wait(barrier, 4 + has_b.astype(jnp.int32) + has_y.astype(jnp.int32) + jnp.where(hub, 12, 0) + jnp.where(is_relay, 2, 0))

    for q in LATE:

        @pl.when(last & (core == q))
        def _():
            above_copy(q).start()

    def start_b():
        pass_on(0, relay_turn < 3)
        b_near(0)
        b_pass(0)

    @pl.when(is_src)
    def _():
        own_piece(2).wait()
        across_copy(2).start()

    def hub_direct():
        @pl.when(hub)
        def _():
            for n in range(2):
                col_copy(0, 1, n, g_a).start()

    row_copy(0, 0).start()

    @pl.when(jnp.logical_not(near))
    def _():
        hub_direct()
        row_copy(0, 1).start()

    @pl.when(is_src)
    def _():
        for q in (5, 4, 3):
            own_piece(q).wait()
            along(q)
        along(2)

    b_far(0)

    def start_cols(s, t):
        g = order(0, t)
        for n in range(2):
            col_copy(s, 0, n, g).start()

        @pl.when(has_y & (jnp.logical_not(hub) | ((t == 3) & (s == 1))))
        def _():
            for n in range(2):
                col_copy(s, 1, n, g).start()

        @pl.when(hub & (t > 0 if s == 0 else t < 3))
        def _():
            for n in range(2):
                hub_copy(s, n, t).start()

    @pl.loop(0, NG)
    def _(t):
        start_cols(0, t)

    def clear_rows(s):
        for n in range(2):
            for p in range(2):
                xs[s, n, p, pl.ds(row_dst[1], W), W : W + TC] = jnp.zeros((W, TC), BF16)

    @pl.when(jnp.logical_not(has_b))
    def _():
        clear_rows(0)

    clear_rows(1)

    @pl.when(jnp.logical_not(has_y))
    def _():
        for s in range(2):
            for n in range(2):
                for p in range(2):
                    xs[s, n, p, :, pl.ds(col_dst[1], W)] = jnp.zeros((TR + 2 * W, W), BF16)

    loads[0].wait()
    loads[1].wait()

    @pl.loop(0, 2 * NG)
    def _(i):
        n, g = i // NG, i % NG
        hi, lo = split(dens[n, pl.ds(mult(g * W), W), :])
        xs[0, n, 0, pl.ds(mult(W + g * W), W), W : W + TC] = hi
        xs[0, n, 1, pl.ds(mult(W + g * W), W), W : W + TC] = lo

    @pl.when(is_src)
    def _():
        @pl.when(first)
        def _():
            take_above()

        for q in LATE:
            own_piece(q).start()
        for q in LATE:
            own_piece(q).wait()
            forward(q)
        row_copy(0, 1).start()
        hub_direct()
        start_b()

    @pl.when(jnp.logical_not(is_src))
    def _():
        for e in range(4):
            q = 2 + jnp.where(near, 3 - e, (dist - e + 4) % 4)
            along_copy(q).wait_recv()
            forward(q)

            @pl.when(goes_across(q))
            def _():
                row_copy(0, 1).start()
                hub_direct()

            @pl.when(e == jnp.where(near, 2, 0))
            def _():
                start_b()

            @pl.when((core == 0) & (e == jnp.where(near, 3, jnp.minimum(dist + 1, 3))))
            def _():
                for p in LATE:
                    along_copy(p).wait_recv()
                    forward(p)

        @pl.when(core == 0)
        def _():
            for p in LATE:
                mate_copy(p).start()

        @pl.when(first)
        def _():
            take_above()

    pass_on(0, relay_turn == 3)

    @pl.loop(0, TR // BS)
    def _(i):
        g, h = i // 2, i % 2
        rows = pl.ds(mult(h * BS, BS), BS)

        def put(pos, value):
            hi, lo = split(value * STEP_TIME)
            cols = pl.ds(mult(pos * BS, BS), BS)
            hrow[0, g, rows, cols] = hi
            hrow[1, g, rows, cols] = lo

        for d in range(-KB, KB + 1):
            u = ext[pl.ds(mult((i + KB + min(d, 0)) * BS, BS), BS), abs(d) * BS : (abs(d) + 1) * BS]
            value = u if d > 0 else u.T if d < 0 else 0.5 * (u + u.T)
            put(h + d + KB, value)
        put((1 - h) * (2 * KB + 1), jnp.zeros((BS, BS), F32))

    @pl.when(jnp.logical_not(is_src) & (core == 1))
    def _():
        for p in LATE:
            mate_copy(p).wait_recv()

    @pl.loop(0, TC // BS)
    def _(i):
        j, h = i // 2, i % 2
        cols = pl.ds(mult(h * BS, BS), BS)

        def put(pos, value):
            hi, lo = split(value * -STEP_TIME)
            rows = pl.ds(mult(pos * BS, BS), BS)
            ncol[0, j, rows, cols] = hi
            ncol[1, j, rows, cols] = lo

        for d in range(-KB, KB + 1):
            u = band[pl.ds(mult((i + KB + min(d, 0)) * BS, BS), BS), abs(d) * BS : (abs(d) + 1) * BS]
            value = u if d < 0 else u.T if d > 0 else 0.5 * (u + u.T)
            put(h + d + KB, value)
        put((1 - h) * (2 * KB + 1), jnp.zeros((BS, BS), F32))

    def take_cols(s, slot, g):
        rows = pl.ds(mult(g * W), W)
        for n in range(2):
            col_copy(s, slot, n, g).wait_recv()
        for n in range(2):
            hi, lo = split(colbuf[s, slot, n, rows, :])
            xs[s, n, 0, pl.ds(mult(W + g * W), W), pl.ds(col_dst[slot], W)] = hi
            xs[s, n, 1, pl.ds(mult(W + g * W), W), pl.ds(col_dst[slot], W)] = lo

    def take_rows(s, slot):
        if slot == 0:
            for n in range(2):
                row_copy(s, n).wait_recv()
        else:
            for i in range(4):
                b_direct(s, i).wait_recv()
        for n in range(2):
            hi, lo = split(rowbuf[s, slot, n])
            xs[s, n, 0, pl.ds(row_dst[slot], W), W : W + TC] = hi
            xs[s, n, 1, pl.ds(row_dst[slot], W), W : W + TC] = lo

    def product(s, n, g, j):
        r0, c0 = mult(g * W), mult(j * W)
        hi, lo = xs.at[s, 1 - n, 0], xs.at[s, 1 - n, 1]
        row_h = hi[pl.ds(r0, 3 * W), pl.ds(mult(c0 + W), W)]
        row_l = lo[pl.ds(r0, 3 * W), pl.ds(mult(c0 + W), W)]
        col_h = hi[pl.ds(mult(r0 + W), W), pl.ds(c0, 3 * W)]
        col_l = lo[pl.ds(mult(r0 + W), W), pl.ds(c0, 3 * W)]
        h_h, h_l = hrow[0, g], hrow[1, g]
        n_h, n_l = ncol[0, j], ncol[1, j]
        lhs = jnp.concatenate([h_h, h_h, h_l, col_h, col_l, col_h], axis=1)
        rhs = jnp.concatenate([row_h, row_l, row_h, n_h, n_h, n_l], axis=0)
        total = jnp.dot(lhs, rhs, preferred_element_type=F32)
        return jnp.where(n == 0, 1.0, -1.0).astype(F32) * total

    def last_part(n):
        g = NG - 1 - g_a
        for i in (2 * n, 2 * n + 1):
            b_direct(1, i).wait_recv()
        hi, lo = split(rowbuf[1, 1, n])
        cols = pl.ds(mult(jnp.where(even, 0, 2 * W)), W)
        h_h, h_l = hrow[0, g, :, cols], hrow[1, g, :, cols]
        lhs = jnp.concatenate([h_h, h_h, h_l], axis=1)
        rhs = jnp.concatenate([hi, lo, hi], axis=0)
        rows = pl.ds(mult(g * W), W)
        dens[1 - n, rows, :] += (-0.5 if n == 0 else 0.5) * jnp.dot(lhs, rhs, preferred_element_type=F32)

    @pl.loop(0, NG)
    def _(t):
        g = order(0, t)
        take_cols(0, 0, g)

        @pl.when(has_y)
        def _():
            take_cols(0, 1, g)

        @pl.when(t == 0)
        def _():
            take_rows(0, 0)

        @pl.when((t == 3) & has_b)
        def _():
            take_rows(0, 1)

        @pl.loop(0, 2 * NJ)
        def _(i):
            n, j = i // NJ, i % NJ
            value = product(0, n, g, j)
            grad[n, pl.ds(mult(g * W), W), pl.ds(mult(j * W), W)] = value
            hi, lo = split(value)
            rows, cols = pl.ds(mult(W + g * W), W), pl.ds(mult(W + j * W), W)
            xs[1, n, 0, rows, cols] = hi
            xs[1, n, 1, rows, cols] = lo

        @pl.when(t == 0)
        def _():
            for n in range(2):
                row_copy(1, n).start()

        start_cols(1, t)

        @pl.when(t == 3)
        def _():
            b_far(1)
            pass_on(1, relay_turn != 2)
            b_near(1, (0,))
            pass_on(1, relay_turn == 2)
            b_near(1, (1, 2))
            b_pass(1)

    def finish(g, j):
        @pl.loop(0, 2)
        def _(n):
            rows, cols = pl.ds(mult(g * W), W), pl.ds(mult(j * W), W)
            dens[n, rows, cols] = dens[n, rows, cols] + grad[n, rows, cols] + 0.5 * product(1, n, g, j)

    @pl.loop(0, NG)
    def _(t):
        g = order(1, t)
        take_cols(1, 0, g)

        @pl.when(t == 2)
        def _():
            take_rows(1, 0)

        finish(g, 1 - core)

    @pl.loop(0, NG)
    def _(t):
        g = order(1, t)

        @pl.when(has_y)
        def _():
            take_cols(1, 1, g)

        finish(g, core)

    @pl.when(has_b)
    def _():
        for n in range(2):
            last_part(n)

    for s in range(2):
        for n in range(2):
            row_copy(s, n).wait_send()

        @pl.when(has_b)
        def _():
            for i in range(4):
                b_direct(s, i).wait_send()

        for i in range(1, 4):

            @pl.when(i > depth)
            def _():
                b_second(s, i).wait_send()

        @pl.loop(0, NG)
        def _(g):
            for n in range(2):
                col_copy(s, 0, n, g).wait_send()

            @pl.when(has_y)
            def _():
                for n in range(2):
                    col_copy(s, 1, n, g).wait_send()

    @pl.when(is_relay)
    def _():
        for s in range(2):
            relay_copy(s).wait_send()

    for q in LATE:

        @pl.when(last & (core == q))
        def _():
            above_copy(q).wait_send()

        @pl.when(first & (core == q))
        def _():
            swap_copy(q).wait_send()

    @pl.when(jnp.logical_not(is_src) & (core == 0))
    def _():
        for p in LATE:
            mate_copy(p).wait_send()

    for q in range(6):

        @pl.when(goes_across(q))
        def _():
            across_copy(q).wait_send()

        @pl.when(goes_back(q))
        def _():
            back_copy(q).wait_send()

        @pl.when(goes_along(q))
        def _():
            along_copy(q).wait_send()


def shards(dens_real, dens_imag, upper_band, pattern):
    dma = pltpu.SemaphoreType.DMA
    anywhere = pl.BlockSpec(memory_space=pl.ANY)
    out = pl.pallas_call(
        kernel,
        out_shape=pltpu.VMEM((2, TR, TC), F32),
        in_specs=[anywhere] * 3 + [pl.BlockSpec(memory_space=pltpu.SMEM)],
        out_specs=pl.BlockSpec(memory_space=pltpu.VMEM),
        scratch_shapes=[
            pltpu.VMEM((2, TR, TC), F32),
            pltpu.VMEM((2, 2, 2, TR + 2 * W, TC + 2 * W), BF16),
            pltpu.VMEM((2, 2, 2, W, TC), F32),
            pltpu.VMEM((2, 2, 2, TR, W), F32),
            pltpu.VMEM((TR + W, 3 * BS), F32),
            pltpu.VMEM((TC + W, 3 * BS), F32),
            pltpu.VMEM((2, NG, W, 3 * W), BF16),
            pltpu.VMEM((2, NJ, 3 * W, W), BF16),
            pltpu.VMEM((2, W, W), F32),
            pltpu.VMEM((2, 4, BS, TC), F32),
            dma((9,)),
            dma((2, 2)),
            dma((2, 2)),
            dma((2, 4)),
            dma((2, 4)),
            dma((2, 4)),
            dma((2, 4)),
            dma((2, 2, 2, NG)),
            dma((2, 2, 2, NG)),
            dma((2,)),
            dma((2,)),
            dma((2,)),
            dma((2,)),
            dma((6,)),
            dma((6,)),
            dma((6,)),
            dma((6,)),
            dma((2,)),
            dma((2,)),
        ],
        compiler_params=pltpu.CompilerParams(collective_id=0, has_side_effects=True, vmem_limit_bytes=55 << 20),
        name="heun",
    )(dens_real, dens_imag, upper_band, pattern.T)
    return out[0], out[1]


def solution(mesh):
    in_specs = (P("row", "col"), P("row", "col"), P("row", None), P("row", None))
    out_specs = (P("row", "col"), P("row", "col"))
    return jax.shard_map(shards, mesh=mesh, in_specs=in_specs, out_specs=out_specs, check_vma=False)
```

```python
import jax
import jax.numpy as jnp
from jax import lax
from jax.experimental import pallas as pl
from jax.experimental.pallas import tpu as pltpu
from jax.sharding import PartitionSpec as P

BS = 128
KB = 2
NB = 64
STEP_TIME = 0.3
MESH = pl.DeviceIdType.MESH
F32 = jnp.float32
BF16 = jnp.bfloat16
TR = 1024
TC = 512
W = KB * BS
NG = TR // W
NJ = TC // W
ROWS = 8
COLS = 16
PIECES = [(0, BS, 2 * BS, BS), (BS, BS, BS, 2 * BS)] + [(q * BS, BS, 0, 3 * BS) for q in range(2, 6)]
LATE = (0, 1)
EARLY = (2, 3, 4, 5)


def mult(x, n=W):
    return pl.multiple_of(x, n)


def split(x):
    hi = x.astype(BF16)
    return hi, (x - hi.astype(F32)).astype(BF16)


def kernel(a_ref, b_ref, u_ref, pat_ref, dens, grad, xs, rowbuf, colbuf, ext, band, hrow, ncol, relay, zrelay,
           lsem, rs_s, rs_r, bs_s, bs_r, bz_s, bz_r, cs_s, cs_r, ab_s, ab_r, sw_s, mt_s, bk_s, al_s, cr_s, bd_r, rl_s, rl_r):
    r, c = lax.axis_index("row"), lax.axis_index("col")
    even, core = r % 2 == 0, c % 2
    k = c // 2
    z, zk, half = r // 2, k // 2, r % 2
    step_up = k % 2 == 0
    dist = jnp.where(step_up, z - zk, zk - z)
    dist = (dist + 4) % 4
    is_src = r == k
    near = half == k % 2
    a_row = jnp.where(even, r + 1, r - 1)
    b_row = jnp.where(even, r - 1, r + 1)
    has_b = (b_row >= 0) & (b_row < ROWS)
    cc_col = jnp.where(core == 0, c + 1, c - 1)
    cy_col = jnp.where(core == 0, c - 1, c + 1)
    has_y = (cy_col >= 0) & (cy_col < COLS)
    hub = (c == 7) | (c == 8)
    mine = jnp.minimum(c, COLS - 1 - c)
    is_relay = mine < 6
    relay_n = mine % 2
    relay_turn = jnp.where(mine < 2, 1, jnp.where(mine < 4, 3, 2))
    relay_to = jnp.where(c < 8, 8, 7)
    urgent = is_src | (r + 1 == k) | (r + 1 == k + 1 - 2 * (k % 2))
    z_up, z_dn = (r + 2) % ROWS, (r + 6) % ROWS
    z_next, z_back = jnp.where(step_up, z_up, z_dn), jnp.where(step_up, z_dn, z_up)
    depth = jnp.where(even, z, 3 - z)
    first_far = depth
    z_relay = jnp.where(even, z_dn, z_up)
    first = r > 0
    last = r < ROWS - 1

    row_dev = ((a_row, c), (b_row, c))
    row_src = (mult(jnp.where(even, TR - W, 0)), mult(jnp.where(even, 0, TR - W)))
    row_dst = (mult(jnp.where(even, TR + W, 0)), mult(jnp.where(even, 0, TR + W)))
    col_dev = ((r, cc_col), (r, cy_col))
    col_src = (mult(jnp.where(core == 0, TC - W, 0)), mult(jnp.where(core == 0, 0, TC - W)))
    col_dst = (mult(jnp.where(core == 0, TC + W, 0)), mult(jnp.where(core == 0, 0, TC + W)))
    g_a = jnp.where(even, NG - 1, 0)
    ext_off = mult(core * TC, BS)

    def order(s, t):
        if s == 0:
            return jnp.where(t == 0, g_a, jnp.where(t == 3, NG - 1 - g_a, t))
        return jnp.where(t < 2, t + 1, jnp.where(t == 2, g_a, NG - 1 - g_a))

    def remote(src, dst, ss, rs, dev):
        return pltpu.make_async_remote_copy(src, dst, ss, rs, device_id=dev, device_id_type=MESH)

    def row_copy(s, n):
        src = (a_ref, b_ref)[n] if s == 0 else grad.at[n]
        return remote(src.at[pl.ds(row_src[0], W), :], rowbuf.at[s, 0, n], rs_s.at[s, n], rs_r.at[s, n], row_dev[0])

    def b_src(s, i):
        src = (a_ref, b_ref)[i // 2] if s == 0 else grad.at[i // 2]
        return src.at[pl.ds(mult(row_src[1] + i % 2 * BS, BS), BS), :]

    def b_dst(s, i):
        return rowbuf.at[s, 1, i // 2, i % 2 * BS : (i % 2 + 1) * BS, :]

    def b_direct(s, i):
        return remote(b_src(s, i), b_dst(s, i), bs_s.at[s, i], bs_r.at[s, i], row_dev[1])

    def b_first(s, i):
        return remote(b_src(s, i), zrelay.at[s, i], bs_s.at[s, i], bz_r.at[s, i], (z_relay, c))

    def b_second(s, i):
        return remote(zrelay.at[s, i], b_dst(s, i), bz_s.at[s, i], bs_r.at[s, i], (a_row, c))

    def b_far(s):
        for i in range(4):

            @pl.when(has_b & (i >= first_far))
            def _():
                b_first(s, i).start()

    def b_near(s, pieces=(0, 1, 2)):
        for i in pieces:

            @pl.when(has_b & (i < first_far))
            def _():
                b_direct(s, i).start()

    def b_pass(s):
        for i in range(1, 4):

            @pl.when(i > depth)
            def _():
                b_first(s, i).wait_recv()
                b_second(s, i).start()

    def col_copy(s, slot, n, g):
        src = (a_ref, b_ref)[n] if s == 0 else grad.at[n]
        rows = pl.ds(mult(g * W), W)
        return remote(src.at[rows, pl.ds(col_src[slot], W)], colbuf.at[s, slot, n, rows, :], cs_s.at[s, slot, n, g], cs_r.at[s, slot, n, g], col_dev[slot])

    def hub_copy(s, n, t):
        g = order(0, t)
        src = (a_ref, b_ref)[n] if s == 0 else grad.at[n]
        turn = t if s == 0 else jnp.where(t == 0, 3, t)
        near_col = jnp.where(turn == 1, 0, jnp.where(turn == 2, 4, 2)) + n
        to = jnp.where(c < 8, near_col, COLS - 1 - near_col)
        return remote(src.at[pl.ds(mult(g * W), W), pl.ds(col_src[1], W)], relay.at[s], cs_s.at[s, 1, n, g], rl_r.at[s], (r, to))

    def relay_copy(s):
        g = order(0, relay_turn if s == 0 else relay_turn % 3)
        return remote(relay.at[s], colbuf.at[s, 1, relay_n, pl.ds(mult(g * W), W), :], rl_s.at[s], cs_r.at[s, 1, relay_n, g], (r, relay_to))

    def pass_on(s, which):
        @pl.when(is_relay & which)
        def _():
            hub_copy(s, 0, 1).wait_recv()
            relay_copy(s).start()

    def above_copy(q):
        r0, nr, c0, nc = PIECES[q]
        return remote(ext.at[TR + r0 : TR + r0 + nr, c0 : c0 + nc], ext.at[r0 : r0 + nr, c0 : c0 + nc], ab_s.at[q], ab_r.at[q], (jnp.minimum(r + 1, ROWS - 1), c))

    def swap_copy(q):
        return remote(piece(ext, q), piece(ext, q), sw_s.at[q], ab_r.at[q], (r, cc_col))

    def take_above():
        for q in LATE:

            @pl.when(core == q)
            def _():
                above_copy(q).wait_recv()
                swap_copy(q).start()
                above_copy(1 - q).wait_recv()


    def piece(ref, q, off=0):
        if isinstance(q, int) and q in LATE:
            r0, nr, c0, nc = PIECES[q]
            return ref.at[pl.ds(mult(off + r0, BS), nr), c0 : c0 + nc]
        return ref.at[pl.ds(mult(off + q * BS, BS), BS), :]

    def part(q):
        return 0 if isinstance(q, int) and q in LATE else q - 2

    def hops(q):
        return (dist - part(q) + 4) % 4

    def travels(q):
        return core == 0 if isinstance(q, int) and q in LATE else True

    def goes_along(q):
        return (jnp.where(near, dist + 1, hops(q)) < 3) & travels(q)

    def goes_across(q):
        return near & (dist == part(q)) & travels(q)

    def goes_back(q):
        return is_src & travels(q)

    def mate_copy(p):
        r0, nr, c0, nc = PIECES[p]
        return remote(band.at[r0 + 4 * BS : r0 + 4 * BS + nr, c0 : c0 + nc], piece(band, p), mt_s.at[p], bd_r.at[p], (r, cc_col))

    def along_copy(q):
        return remote(piece(band, q), piece(band, q), al_s.at[q], bd_r.at[q], (z_next, c))

    def across_copy(q):
        return remote(piece(band, q), piece(band, q), cr_s.at[q], bd_r.at[q], (a_row, c))

    def back_copy(q):
        return remote(piece(band, q), piece(band, q), bk_s.at[q], bd_r.at[q], (z_back, c))

    def along(q):
        @pl.when(goes_back(q))
        def _():
            back_copy(q).start()

        @pl.when(goes_along(q))
        def _():
            along_copy(q).start()

    def forward(q):
        @pl.when(goes_across(q))
        def _():
            across_copy(q).start()

        along(q)

    def own_piece(q):
        return pltpu.make_async_copy(piece(ext, q, ext_off), piece(band, q), lsem.at[3 + q])

    barrier = pltpu.get_barrier_semaphore()

    def greet(dev):
        pl.semaphore_signal(barrier, inc=1, device_id=dev, device_id_type=MESH)

    for dev in (row_dev[0], col_dev[0], (z_up, c), (z_dn, c)):
        greet(dev)

    @pl.when(has_b)
    def _():
        greet(row_dev[1])

    @pl.when(has_y)
    def _():
        greet(col_dev[1])

    loads = [
        pltpu.make_async_copy(a_ref, dens.at[0], lsem.at[0]),
        pltpu.make_async_copy(b_ref, dens.at[1], lsem.at[1]),
        pltpu.make_async_copy(u_ref, ext.at[W:, :], lsem.at[2]),
    ]

    for cp in loads[::-1]:
        cp.start()

    @pl.when(jnp.logical_not(first))
    def _():
        ext[0:W, :] = jnp.zeros((W, 3 * BS), F32)

    def prepare():
        loads[2].wait()

        @pl.loop(0, TR // BS)
        def _(i):
            rows = pl.ds(mult(W + i * BS, BS), BS)
            for d in range(1, KB + 1):
                present = (pat_ref[d - 1, i] > 0) & (r * (TR // BS) + i + d < NB)
                cols = slice(d * BS, (d + 1) * BS)
                ext[rows, cols] = ext[rows, cols] * jnp.where(present, 1.0, 0.0).astype(F32)

    @pl.when(urgent)
    def _():
        prepare()

    @pl.when(is_src)
    def _():
        for q in EARLY:
            own_piece(q).start()

    @pl.when(hub)
    def _():
        for col in (*range(6), *range(10, COLS)):
            greet((r, col))

    @pl.when(is_relay)
    def _():
        for col in (7, 8):
            greet((r, col))

    pl.semaphore_wait(barrier, 4 + has_b.astype(jnp.int32) + has_y.astype(jnp.int32) + jnp.where(hub, 12, 0) + jnp.where(is_relay, 2, 0))

    def start_above():
        for q in LATE:

            @pl.when(last & (core == q))
            def _():
                above_copy(q).start()

    @pl.when(urgent)
    def _():
        start_above()

    def start_b():
        pass_on(0, relay_turn < 3)
        b_near(0)
        b_pass(0)

    @pl.when(is_src)
    def _():
        own_piece(2).wait()
        across_copy(2).start()

    def hub_direct():
        @pl.when(hub)
        def _():
            for n in range(2):
                col_copy(0, 1, n, g_a).start()

    row_copy(0, 0).start()

    @pl.when(jnp.logical_not(near))
    def _():
        hub_direct()
        row_copy(0, 1).start()

    @pl.when(is_src)
    def _():
        for q in (5, 4, 3):
            own_piece(q).wait()
            along(q)
        along(2)

    b_far(0)

    def start_cols(s, t):
        g = order(0, t)
        for n in range(2):
            col_copy(s, 0, n, g).start()

        @pl.when(has_y & (jnp.logical_not(hub) | ((t == 3) & (s == 1))))
        def _():
            for n in range(2):
                col_copy(s, 1, n, g).start()

        @pl.when(hub & (t > 0 if s == 0 else t < 3))
        def _():
            for n in range(2):
                hub_copy(s, n, t).start()

    @pl.loop(0, NG)
    def _(t):
        start_cols(0, t)

    @pl.when(jnp.logical_not(urgent))
    def _():
        prepare()
        start_above()

    def clear_rows(s):
        for n in range(2):
            for p in range(2):
                xs[s, n, p, pl.ds(row_dst[1], W), W : W + TC] = jnp.zeros((W, TC), BF16)

    @pl.when(jnp.logical_not(has_b))
    def _():
        clear_rows(0)

    clear_rows(1)

    @pl.when(jnp.logical_not(has_y))
    def _():
        for s in range(2):
            for n in range(2):
                for p in range(2):
                    xs[s, n, p, :, pl.ds(col_dst[1], W)] = jnp.zeros((TR + 2 * W, W), BF16)

    loads[0].wait()
    loads[1].wait()

    @pl.loop(0, 2 * NG)
    def _(i):
        n, g = i // NG, i % NG
        hi, lo = split(dens[n, pl.ds(mult(g * W), W), :])
        xs[0, n, 0, pl.ds(mult(W + g * W), W), W : W + TC] = hi
        xs[0, n, 1, pl.ds(mult(W + g * W), W), W : W + TC] = lo

    @pl.when(is_src)
    def _():
        @pl.when(first)
        def _():
            take_above()

        for q in LATE:
            own_piece(q).start()
        for q in LATE:
            own_piece(q).wait()
            forward(q)
        row_copy(0, 1).start()
        hub_direct()
        start_b()

    def build_rows():
        @pl.loop(0, TR // BS)
        def _(i):
            g, h = i // 2, i % 2
            rows = pl.ds(mult(h * BS, BS), BS)

            def put(pos, value):
                hi, lo = split(value * STEP_TIME)
                cols = pl.ds(mult(pos * BS, BS), BS)
                hrow[0, g, rows, cols] = hi
                hrow[1, g, rows, cols] = lo

            for d in range(-KB, KB + 1):
                u = ext[pl.ds(mult((i + KB + min(d, 0)) * BS, BS), BS), abs(d) * BS : (abs(d) + 1) * BS]
                value = u if d > 0 else u.T if d < 0 else 0.5 * (u + u.T)
                put(h + d + KB, value)
            put((1 - h) * (2 * KB + 1), jnp.zeros((BS, BS), F32))

    @pl.when(jnp.logical_not(near))
    def _():
        @pl.when(first)
        def _():
            take_above()

        build_rows()

    @pl.when(jnp.logical_not(is_src))
    def _():
        for e in range(4):
            q = 2 + jnp.where(near, 3 - e, (dist - e + 4) % 4)
            along_copy(q).wait_recv()
            forward(q)

            @pl.when(goes_across(q))
            def _():
                row_copy(0, 1).start()
                hub_direct()

            @pl.when(e == jnp.where(near, 2, 0))
            def _():
                start_b()

            @pl.when((core == 0) & (e == jnp.where(near, 3, dist)))
            def _():
                for p in LATE:
                    along_copy(p).wait_recv()
                    forward(p)

        @pl.when(core == 0)
        def _():
            for p in LATE:
                mate_copy(p).start()

        @pl.when(first & near)
        def _():
            take_above()

    pass_on(0, relay_turn == 3)

    @pl.when(near)
    def _():
        build_rows()

    @pl.when(jnp.logical_not(is_src) & (core == 1))
    def _():
        for p in LATE:
            mate_copy(p).wait_recv()

    @pl.loop(0, TC // BS)
    def _(i):
        j, h = i // 2, i % 2
        cols = pl.ds(mult(h * BS, BS), BS)

        def put(pos, value):
            hi, lo = split(value * -STEP_TIME)
            rows = pl.ds(mult(pos * BS, BS), BS)
            ncol[0, j, rows, cols] = hi
            ncol[1, j, rows, cols] = lo

        for d in range(-KB, KB + 1):
            u = band[pl.ds(mult((i + KB + min(d, 0)) * BS, BS), BS), abs(d) * BS : (abs(d) + 1) * BS]
            value = u if d < 0 else u.T if d > 0 else 0.5 * (u + u.T)
            put(h + d + KB, value)
        put((1 - h) * (2 * KB + 1), jnp.zeros((BS, BS), F32))

    def take_cols(s, slot, g):
        rows = pl.ds(mult(g * W), W)
        for n in range(2):
            col_copy(s, slot, n, g).wait_recv()
        for n in range(2):
            hi, lo = split(colbuf[s, slot, n, rows, :])
            xs[s, n, 0, pl.ds(mult(W + g * W), W), pl.ds(col_dst[slot], W)] = hi
            xs[s, n, 1, pl.ds(mult(W + g * W), W), pl.ds(col_dst[slot], W)] = lo

    def take_rows(s, slot):
        if slot == 0:
            for n in range(2):
                row_copy(s, n).wait_recv()
        else:
            for i in range(4):
                b_direct(s, i).wait_recv()
        for n in range(2):
            hi, lo = split(rowbuf[s, slot, n])
            xs[s, n, 0, pl.ds(row_dst[slot], W), W : W + TC] = hi
            xs[s, n, 1, pl.ds(row_dst[slot], W), W : W + TC] = lo

    def product(s, n, g, j):
        r0, c0 = mult(g * W), mult(j * W)
        hi, lo = xs.at[s, 1 - n, 0], xs.at[s, 1 - n, 1]
        row_h = hi[pl.ds(r0, 3 * W), pl.ds(mult(c0 + W), W)]
        row_l = lo[pl.ds(r0, 3 * W), pl.ds(mult(c0 + W), W)]
        col_h = hi[pl.ds(mult(r0 + W), W), pl.ds(c0, 3 * W)]
        col_l = lo[pl.ds(mult(r0 + W), W), pl.ds(c0, 3 * W)]
        h_h, h_l = hrow[0, g], hrow[1, g]
        n_h, n_l = ncol[0, j], ncol[1, j]
        lhs = jnp.concatenate([h_h, h_h, h_l, col_h, col_l, col_h], axis=1)
        rhs = jnp.concatenate([row_h, row_l, row_h, n_h, n_h, n_l], axis=0)
        total = jnp.dot(lhs, rhs, preferred_element_type=F32)
        return jnp.where(n == 0, 1.0, -1.0).astype(F32) * total

    def last_part(n):
        g = NG - 1 - g_a
        for i in (2 * n, 2 * n + 1):
            b_direct(1, i).wait_recv()
        hi, lo = split(rowbuf[1, 1, n])
        cols = pl.ds(mult(jnp.where(even, 0, 2 * W)), W)
        h_h, h_l = hrow[0, g, :, cols], hrow[1, g, :, cols]
        lhs = jnp.concatenate([h_h, h_h, h_l], axis=1)
        rhs = jnp.concatenate([hi, lo, hi], axis=0)
        rows = pl.ds(mult(g * W), W)
        dens[1 - n, rows, :] += (-0.5 if n == 0 else 0.5) * jnp.dot(lhs, rhs, preferred_element_type=F32)

    @pl.loop(0, NG)
    def _(t):
        g = order(0, t)
        take_cols(0, 0, g)

        @pl.when(has_y)
        def _():
            take_cols(0, 1, g)

        @pl.when(t == 0)
        def _():
            take_rows(0, 0)

        @pl.when((t == 3) & has_b)
        def _():
            take_rows(0, 1)

        @pl.loop(0, 2 * NJ)
        def _(i):
            n, j = i // NJ, i % NJ
            value = product(0, n, g, j)
            grad[n, pl.ds(mult(g * W), W), pl.ds(mult(j * W), W)] = value
            hi, lo = split(value)
            rows, cols = pl.ds(mult(W + g * W), W), pl.ds(mult(W + j * W), W)
            xs[1, n, 0, rows, cols] = hi
            xs[1, n, 1, rows, cols] = lo
            for m in range(2):

                @pl.when((t == 0) & (i == (m + 1) * NJ - 1))
                def _():
                    row_copy(1, m).start()

        start_cols(1, t)

        @pl.when(t == 3)
        def _():
            b_far(1)
            pass_on(1, relay_turn != 2)
            b_near(1, (0,))
            pass_on(1, relay_turn == 2)
            b_near(1, (1, 2))
            b_pass(1)

    def finish(g, j):
        @pl.loop(0, 2)
        def _(n):
            rows, cols = pl.ds(mult(g * W), W), pl.ds(mult(j * W), W)
            dens[n, rows, cols] = dens[n, rows, cols] + grad[n, rows, cols] + 0.5 * product(1, n, g, j)

    @pl.loop(0, NG)
    def _(t):
        g = order(1, t)
        take_cols(1, 0, g)

        @pl.when(t == 2)
        def _():
            take_rows(1, 0)

        finish(g, 1 - core)

    @pl.loop(0, NG)
    def _(t):
        g = order(1, t)

        @pl.when(has_y)
        def _():
            take_cols(1, 1, g)

        finish(g, core)

    @pl.when(has_b)
    def _():
        for n in range(2):
            last_part(n)

    for s in range(2):
        for n in range(2):
            row_copy(s, n).wait_send()

        @pl.when(has_b)
        def _():
            for i in range(4):
                b_direct(s, i).wait_send()

        for i in range(1, 4):

            @pl.when(i > depth)
            def _():
                b_second(s, i).wait_send()

        @pl.loop(0, NG)
        def _(g):
            for n in range(2):
                col_copy(s, 0, n, g).wait_send()

            @pl.when(has_y)
            def _():
                for n in range(2):
                    col_copy(s, 1, n, g).wait_send()

    @pl.when(is_relay)
    def _():
        for s in range(2):
            relay_copy(s).wait_send()

    for q in LATE:

        @pl.when(last & (core == q))
        def _():
            above_copy(q).wait_send()

        @pl.when(first & (core == q))
        def _():
            swap_copy(q).wait_send()

    @pl.when(jnp.logical_not(is_src) & (core == 0))
    def _():
        for p in LATE:
            mate_copy(p).wait_send()

    for q in range(6):

        @pl.when(goes_across(q))
        def _():
            across_copy(q).wait_send()

        @pl.when(goes_back(q))
        def _():
            back_copy(q).wait_send()

        @pl.when(goes_along(q))
        def _():
            along_copy(q).wait_send()


def shards(dens_real, dens_imag, upper_band, pattern):
    dma = pltpu.SemaphoreType.DMA
    anywhere = pl.BlockSpec(memory_space=pl.ANY)
    out = pl.pallas_call(
        kernel,
        out_shape=pltpu.VMEM((2, TR, TC), F32),
        in_specs=[anywhere] * 3 + [pl.BlockSpec(memory_space=pltpu.SMEM)],
        out_specs=pl.BlockSpec(memory_space=pltpu.VMEM),
        scratch_shapes=[
            pltpu.VMEM((2, TR, TC), F32),
            pltpu.VMEM((2, 2, 2, TR + 2 * W, TC + 2 * W), BF16),
            pltpu.VMEM((2, 2, 2, W, TC), F32),
            pltpu.VMEM((2, 2, 2, TR, W), F32),
            pltpu.VMEM((TR + W, 3 * BS), F32),
            pltpu.VMEM((TC + W, 3 * BS), F32),
            pltpu.VMEM((2, NG, W, 3 * W), BF16),
            pltpu.VMEM((2, NJ, 3 * W, W), BF16),
            pltpu.VMEM((2, W, W), F32),
            pltpu.VMEM((2, 4, BS, TC), F32),
            dma((9,)),
            dma((2, 2)),
            dma((2, 2)),
            dma((2, 4)),
            dma((2, 4)),
            dma((2, 4)),
            dma((2, 4)),
            dma((2, 2, 2, NG)),
            dma((2, 2, 2, NG)),
            dma((2,)),
            dma((2,)),
            dma((2,)),
            dma((2,)),
            dma((6,)),
            dma((6,)),
            dma((6,)),
            dma((6,)),
            dma((2,)),
            dma((2,)),
        ],
        compiler_params=pltpu.CompilerParams(collective_id=0, has_side_effects=True, vmem_limit_bytes=55 << 20),
        name="heun",
    )(dens_real, dens_imag, upper_band, pattern.T)
    return out[0], out[1]


def solution(mesh):
    in_specs = (P("row", "col"), P("row", "col"), P("row", None), P("row", None))
    out_specs = (P("row", "col"), P("row", "col"))
    return jax.shard_map(shards, mesh=mesh, in_specs=in_specs, out_specs=out_specs, check_vma=False)
```

```python
import jax
import jax.numpy as jnp
from jax import lax
from jax.experimental import pallas as pl
from jax.experimental.pallas import tpu as pltpu
from jax.sharding import PartitionSpec as P

BS = 128
KB = 2
NB = 64
STEP_TIME = 0.3
MESH = pl.DeviceIdType.MESH
F32 = jnp.float32
BF16 = jnp.bfloat16
TR = 1024
TC = 512
W = KB * BS
NG = TR // W
NJ = TC // W
ROWS = 8
COLS = 16
PIECES = [(0, BS, 2 * BS, BS), (BS, BS, BS, 2 * BS)] + [(q * BS, BS, 0, 3 * BS) for q in range(2, 6)]
LATE = (0, 1)
EARLY = (2, 3, 4, 5)


def mult(x, n=W):
    return pl.multiple_of(x, n)


def split(x):
    hi = x.astype(BF16)
    return hi, (x - hi.astype(F32)).astype(BF16)


def kernel(a_ref, b_ref, u_ref, pat_ref, dens, grad, xs, rowbuf, colbuf, ext, band, hrow, ncol, relay, zrelay,
           lsem, rs_s, rs_r, bs_s, bs_r, bz_s, bz_r, cs_s, cs_r, ab_s, ab_r, sw_s, mt_s, bk_s, al_s, cr_s, bd_r, rl_s, rl_r):
    r, c = lax.axis_index("row"), lax.axis_index("col")
    even, core = r % 2 == 0, c % 2
    k = c // 2
    z, zk, half = r // 2, k // 2, r % 2
    step_up = k % 2 == 0
    dist = jnp.where(step_up, z - zk, zk - z)
    dist = (dist + 4) % 4
    is_src = r == k
    near = half == k % 2
    a_row = jnp.where(even, r + 1, r - 1)
    b_row = jnp.where(even, r - 1, r + 1)
    has_b = (b_row >= 0) & (b_row < ROWS)
    cc_col = jnp.where(core == 0, c + 1, c - 1)
    cy_col = jnp.where(core == 0, c - 1, c + 1)
    has_y = (cy_col >= 0) & (cy_col < COLS)
    hub = (c == 7) | (c == 8)
    mine = jnp.minimum(c, COLS - 1 - c)
    is_relay = mine < 6
    relay_n = mine % 2
    relay_turn = jnp.where(mine < 2, 1, jnp.where(mine < 4, 3, 2))
    relay_to = jnp.where(c < 8, 8, 7)
    urgent = is_src | (r + 1 == k) | (r + 1 == k + 1 - 2 * (k % 2))
    z_up, z_dn = (r + 2) % ROWS, (r + 6) % ROWS
    z_next, z_back = jnp.where(step_up, z_up, z_dn), jnp.where(step_up, z_dn, z_up)
    depth = jnp.where(even, z, 3 - z)
    first_far = depth
    z_relay = jnp.where(even, z_dn, z_up)
    first = r > 0
    last = r < ROWS - 1

    row_dev = ((a_row, c), (b_row, c))
    row_src = (mult(jnp.where(even, TR - W, 0)), mult(jnp.where(even, 0, TR - W)))
    row_dst = (mult(jnp.where(even, TR + W, 0)), mult(jnp.where(even, 0, TR + W)))
    col_dev = ((r, cc_col), (r, cy_col))
    col_src = (mult(jnp.where(core == 0, TC - W, 0)), mult(jnp.where(core == 0, 0, TC - W)))
    col_dst = (mult(jnp.where(core == 0, TC + W, 0)), mult(jnp.where(core == 0, 0, TC + W)))
    g_a = jnp.where(even, NG - 1, 0)
    ext_off = mult(core * TC, BS)

    def order(s, t):
        if s == 0:
            return jnp.where(t == 0, g_a, jnp.where(t == 3, NG - 1 - g_a, t))
        return jnp.where(t < 2, t + 1, jnp.where(t == 2, g_a, NG - 1 - g_a))

    def remote(src, dst, ss, rs, dev):
        return pltpu.make_async_remote_copy(src, dst, ss, rs, device_id=dev, device_id_type=MESH)

    def row_copy(s, n):
        src = (a_ref, b_ref)[n] if s == 0 else grad.at[n]
        return remote(src.at[pl.ds(row_src[0], W), :], rowbuf.at[s, 0, n], rs_s.at[s, n], rs_r.at[s, n], row_dev[0])

    def b_src(s, i):
        src = (a_ref, b_ref)[i // 2] if s == 0 else grad.at[i // 2]
        return src.at[pl.ds(mult(row_src[1] + i % 2 * BS, BS), BS), :]

    def b_dst(s, i):
        return rowbuf.at[s, 1, i // 2, i % 2 * BS : (i % 2 + 1) * BS, :]

    def b_direct(s, i):
        return remote(b_src(s, i), b_dst(s, i), bs_s.at[s, i], bs_r.at[s, i], row_dev[1])

    def b_first(s, i):
        return remote(b_src(s, i), zrelay.at[s, i], bs_s.at[s, i], bz_r.at[s, i], (z_relay, c))

    def b_second(s, i):
        return remote(zrelay.at[s, i], b_dst(s, i), bz_s.at[s, i], bs_r.at[s, i], (a_row, c))

    def b_far(s):
        for i in range(4):

            @pl.when(has_b & (i >= first_far))
            def _():
                b_first(s, i).start()

    def b_near(s, pieces=(0, 1, 2)):
        for i in pieces:

            @pl.when(has_b & (i < first_far))
            def _():
                b_direct(s, i).start()

    def b_pass(s):
        for i in range(1, 4):

            @pl.when(i > depth)
            def _():
                b_first(s, i).wait_recv()
                b_second(s, i).start()

    def col_copy(s, slot, n, g):
        src = (a_ref, b_ref)[n] if s == 0 else grad.at[n]
        rows = pl.ds(mult(g * W), W)
        return remote(src.at[rows, pl.ds(col_src[slot], W)], colbuf.at[s, slot, n, rows, :], cs_s.at[s, slot, n, g], cs_r.at[s, slot, n, g], col_dev[slot])

    def hub_copy(s, n, t):
        g = order(0, t)
        src = (a_ref, b_ref)[n] if s == 0 else grad.at[n]
        turn = t if s == 0 else jnp.where(t == 0, 3, t)
        near_col = jnp.where(turn == 1, 0, jnp.where(turn == 2, 4, 2)) + n
        to = jnp.where(c < 8, near_col, COLS - 1 - near_col)
        return remote(src.at[pl.ds(mult(g * W), W), pl.ds(col_src[1], W)], relay.at[s], cs_s.at[s, 1, n, g], rl_r.at[s], (r, to))

    def relay_copy(s):
        g = order(0, relay_turn if s == 0 else relay_turn % 3)
        return remote(relay.at[s], colbuf.at[s, 1, relay_n, pl.ds(mult(g * W), W), :], rl_s.at[s], cs_r.at[s, 1, relay_n, g], (r, relay_to))

    def pass_on(s, which):
        @pl.when(is_relay & which)
        def _():
            hub_copy(s, 0, 1).wait_recv()
            relay_copy(s).start()

    def above_copy(q):
        r0, nr, c0, nc = PIECES[q]
        return remote(ext.at[TR + r0 : TR + r0 + nr, c0 : c0 + nc], ext.at[r0 : r0 + nr, c0 : c0 + nc], ab_s.at[q], ab_r.at[q], (jnp.minimum(r + 1, ROWS - 1), c))

    def swap_copy(q):
        return remote(piece(ext, q), piece(ext, q), sw_s.at[q], ab_r.at[q], (r, cc_col))

    def take_above():
        for q in LATE:

            @pl.when(core == q)
            def _():
                above_copy(q).wait_recv()
                swap_copy(q).start()
                above_copy(1 - q).wait_recv()


    def piece(ref, q, off=0):
        if isinstance(q, int) and q in LATE:
            r0, nr, c0, nc = PIECES[q]
            return ref.at[pl.ds(mult(off + r0, BS), nr), c0 : c0 + nc]
        return ref.at[pl.ds(mult(off + q * BS, BS), BS), :]

    def part(q):
        return 0 if isinstance(q, int) and q in LATE else q - 2

    def hops(q):
        return (dist - part(q) + 4) % 4

    def travels(q):
        return core == 0 if isinstance(q, int) and q in LATE else True

    def goes_along(q):
        return (jnp.where(near, dist + 1, hops(q)) < 3) & travels(q)

    def goes_across(q):
        return near & (dist == part(q)) & travels(q)

    def goes_back(q):
        return is_src & travels(q)

    def mate_copy(p):
        r0, nr, c0, nc = PIECES[p]
        return remote(band.at[r0 + 4 * BS : r0 + 4 * BS + nr, c0 : c0 + nc], piece(band, p), mt_s.at[p], bd_r.at[p], (r, cc_col))

    def along_copy(q):
        return remote(piece(band, q), piece(band, q), al_s.at[q], bd_r.at[q], (z_next, c))

    def across_copy(q):
        return remote(piece(band, q), piece(band, q), cr_s.at[q], bd_r.at[q], (a_row, c))

    def back_copy(q):
        return remote(piece(band, q), piece(band, q), bk_s.at[q], bd_r.at[q], (z_back, c))

    def along(q):
        @pl.when(goes_back(q))
        def _():
            back_copy(q).start()

        @pl.when(goes_along(q))
        def _():
            along_copy(q).start()

    def forward(q):
        @pl.when(goes_across(q))
        def _():
            across_copy(q).start()

        along(q)

    def own_piece(q):
        return pltpu.make_async_copy(piece(ext, q, ext_off), piece(band, q), lsem.at[3 + q])

    barrier = pltpu.get_barrier_semaphore()

    def greet(dev):
        pl.semaphore_signal(barrier, inc=1, device_id=dev, device_id_type=MESH)

    for dev in (row_dev[0], col_dev[0], (z_up, c), (z_dn, c)):
        greet(dev)

    @pl.when(has_b)
    def _():
        greet(row_dev[1])

    @pl.when(has_y)
    def _():
        greet(col_dev[1])

    loads = [
        pltpu.make_async_copy(a_ref, dens.at[0], lsem.at[0]),
        pltpu.make_async_copy(b_ref, dens.at[1], lsem.at[1]),
        pltpu.make_async_copy(u_ref, ext.at[W:, :], lsem.at[2]),
    ]

    for cp in loads[::-1]:
        cp.start()

    @pl.when(jnp.logical_not(first))
    def _():
        ext[0:W, :] = jnp.zeros((W, 3 * BS), F32)

    def prepare():
        loads[2].wait()

        @pl.loop(0, TR // BS)
        def _(i):
            rows = pl.ds(mult(W + i * BS, BS), BS)
            for d in range(1, KB + 1):
                present = (pat_ref[d - 1, i] > 0) & (r * (TR // BS) + i + d < NB)
                cols = slice(d * BS, (d + 1) * BS)
                ext[rows, cols] = ext[rows, cols] * jnp.where(present, 1.0, 0.0).astype(F32)

    @pl.when(urgent)
    def _():
        prepare()

    @pl.when(is_src)
    def _():
        for q in EARLY:
            own_piece(q).start()

    @pl.when(hub)
    def _():
        for col in (*range(6), *range(10, COLS)):
            greet((r, col))

    @pl.when(is_relay)
    def _():
        for col in (7, 8):
            greet((r, col))

    pl.semaphore_wait(barrier, 4 + has_b.astype(jnp.int32) + has_y.astype(jnp.int32) + jnp.where(hub, 12, 0) + jnp.where(is_relay, 2, 0))

    def start_above():
        for q in LATE:

            @pl.when(last & (core == q))
            def _():
                above_copy(q).start()

    @pl.when(urgent)
    def _():
        start_above()

    def start_b():
        pass_on(0, relay_turn < 3)
        b_near(0)
        b_pass(0)

    @pl.when(is_src)
    def _():
        own_piece(2).wait()
        across_copy(2).start()

    def hub_direct():
        @pl.when(hub)
        def _():
            for n in range(2):
                col_copy(0, 1, n, g_a).start()

    row_copy(0, 0).start()

    @pl.when(jnp.logical_not(near))
    def _():
        hub_direct()
        row_copy(0, 1).start()

    @pl.when(is_src)
    def _():
        for q in (5, 4, 3):
            own_piece(q).wait()
            along(q)
        along(2)

    b_far(0)

    def start_cols(s, t):
        g = order(0, t)
        for n in range(2):
            col_copy(s, 0, n, g).start()

        @pl.when(has_y & (jnp.logical_not(hub) | ((t == 3) & (s == 1))))
        def _():
            for n in range(2):
                col_copy(s, 1, n, g).start()

        @pl.when(hub & (t > 0 if s == 0 else t < 3))
        def _():
            for n in range(2):
                hub_copy(s, n, t).start()

    @pl.loop(0, NG)
    def _(t):
        start_cols(0, t)

    @pl.when(jnp.logical_not(urgent))
    def _():
        prepare()
        start_above()

    def clear_rows(s):
        for n in range(2):
            for p in range(2):
                xs[s, n, p, pl.ds(row_dst[1], W), W : W + TC] = jnp.zeros((W, TC), BF16)

    @pl.when(jnp.logical_not(has_b))
    def _():
        clear_rows(0)

    clear_rows(1)

    @pl.when(jnp.logical_not(has_y))
    def _():
        for s in range(2):
            for n in range(2):
                for p in range(2):
                    xs[s, n, p, :, pl.ds(col_dst[1], W)] = jnp.zeros((TR + 2 * W, W), BF16)

    loads[0].wait()
    loads[1].wait()

    @pl.loop(0, 2 * NG)
    def _(i):
        n, g = i // NG, i % NG
        hi, lo = split(dens[n, pl.ds(mult(g * W), W), :])
        xs[0, n, 0, pl.ds(mult(W + g * W), W), W : W + TC] = hi
        xs[0, n, 1, pl.ds(mult(W + g * W), W), W : W + TC] = lo

    @pl.when(is_src)
    def _():
        @pl.when(first)
        def _():
            take_above()

        for q in LATE:
            own_piece(q).start()
        for q in LATE:
            own_piece(q).wait()
            forward(q)
        row_copy(0, 1).start()
        hub_direct()
        start_b()

    def build_rows():
        @pl.loop(0, TR // BS)
        def _(i):
            g, h = i // 2, i % 2
            rows = pl.ds(mult(h * BS, BS), BS)

            def put(pos, value):
                hi, lo = split(value * STEP_TIME)
                cols = pl.ds(mult(pos * BS, BS), BS)
                hrow[0, g, rows, cols] = hi
                hrow[1, g, rows, cols] = lo

            for d in range(-KB, KB + 1):
                u = ext[pl.ds(mult((i + KB + min(d, 0)) * BS, BS), BS), abs(d) * BS : (abs(d) + 1) * BS]
                value = u if d > 0 else u.T if d < 0 else 0.5 * (u + u.T)
                put(h + d + KB, value)
            put((1 - h) * (2 * KB + 1), jnp.zeros((BS, BS), F32))

    @pl.when(jnp.logical_not(near))
    def _():
        @pl.when(first)
        def _():
            take_above()

        build_rows()

    @pl.when(jnp.logical_not(is_src))
    def _():
        for e in range(4):
            q = 2 + jnp.where(near, 3 - e, (dist - e + 4) % 4)
            along_copy(q).wait_recv()
            forward(q)

            @pl.when(goes_across(q))
            def _():
                row_copy(0, 1).start()
                hub_direct()

            @pl.when(e == jnp.where(near, 2, 0))
            def _():
                start_b()

            @pl.when((core == 0) & (e == jnp.where(near, 3, dist)))
            def _():
                for p in LATE:
                    along_copy(p).wait_recv()
                    forward(p)

        @pl.when(core == 0)
        def _():
            for p in LATE:
                mate_copy(p).start()

        @pl.when(first & near)
        def _():
            take_above()

    pass_on(0, relay_turn == 3)

    @pl.when(near)
    def _():
        build_rows()

    @pl.when(jnp.logical_not(is_src) & (core == 1))
    def _():
        for p in LATE:
            mate_copy(p).wait_recv()

    @pl.loop(0, TC // BS)
    def _(i):
        j, h = i // 2, i % 2
        cols = pl.ds(mult(h * BS, BS), BS)

        def put(pos, value):
            hi, lo = split(value * -STEP_TIME)
            rows = pl.ds(mult(pos * BS, BS), BS)
            ncol[0, j, rows, cols] = hi
            ncol[1, j, rows, cols] = lo

        for d in range(-KB, KB + 1):
            u = band[pl.ds(mult((i + KB + min(d, 0)) * BS, BS), BS), abs(d) * BS : (abs(d) + 1) * BS]
            value = u if d < 0 else u.T if d > 0 else 0.5 * (u + u.T)
            put(h + d + KB, value)
        put((1 - h) * (2 * KB + 1), jnp.zeros((BS, BS), F32))

    def take_cols(s, slot, g):
        rows = pl.ds(mult(g * W), W)
        for n in range(2):
            col_copy(s, slot, n, g).wait_recv()
        for n in range(2):
            hi, lo = split(colbuf[s, slot, n, rows, :])
            xs[s, n, 0, pl.ds(mult(W + g * W), W), pl.ds(col_dst[slot], W)] = hi
            xs[s, n, 1, pl.ds(mult(W + g * W), W), pl.ds(col_dst[slot], W)] = lo

    def take_rows(s, slot):
        if slot == 0:
            for n in range(2):
                row_copy(s, n).wait_recv()
        else:
            for i in range(4):
                b_direct(s, i).wait_recv()
        for n in range(2):
            hi, lo = split(rowbuf[s, slot, n])
            xs[s, n, 0, pl.ds(row_dst[slot], W), W : W + TC] = hi
            xs[s, n, 1, pl.ds(row_dst[slot], W), W : W + TC] = lo

    def product(s, n, g, j):
        r0, c0 = mult(g * W), mult(j * W)
        hi, lo = xs.at[s, 1 - n, 0], xs.at[s, 1 - n, 1]
        row_h = hi[pl.ds(r0, 3 * W), pl.ds(mult(c0 + W), W)]
        row_l = lo[pl.ds(r0, 3 * W), pl.ds(mult(c0 + W), W)]
        col_h = hi[pl.ds(mult(r0 + W), W), pl.ds(c0, 3 * W)]
        col_l = lo[pl.ds(mult(r0 + W), W), pl.ds(c0, 3 * W)]
        h_h, h_l = hrow[0, g], hrow[1, g]
        n_h, n_l = ncol[0, j], ncol[1, j]
        lhs = jnp.concatenate([h_h, h_h, h_l, col_h, col_l, col_h], axis=1)
        rhs = jnp.concatenate([row_h, row_l, row_h, n_h, n_h, n_l], axis=0)
        total = jnp.dot(lhs, rhs, preferred_element_type=F32)
        return jnp.where(n == 0, 1.0, -1.0).astype(F32) * total

    def last_part(i):
        g, n = NG - 1 - g_a, i // 2
        b_direct(1, i).wait_recv()
        hi, lo = split(rowbuf[1, 1, n, i % 2 * BS : (i % 2 + 1) * BS, :])
        cols = pl.ds(mult(jnp.where(even, 0, 2 * W) + i % 2 * BS, BS), BS)
        h_h, h_l = hrow[0, g, :, cols], hrow[1, g, :, cols]
        lhs = jnp.concatenate([h_h, h_h, h_l], axis=1)
        rhs = jnp.concatenate([hi, lo, hi], axis=0)
        rows = pl.ds(mult(g * W), W)
        dens[1 - n, rows, :] += (-0.5 if n == 0 else 0.5) * jnp.dot(lhs, rhs, preferred_element_type=F32)

    @pl.loop(0, NG)
    def _(t):
        g = order(0, t)
        take_cols(0, 0, g)

        @pl.when(has_y)
        def _():
            take_cols(0, 1, g)

        @pl.when(t == 0)
        def _():
            take_rows(0, 0)

        @pl.when((t == 3) & has_b)
        def _():
            take_rows(0, 1)

        @pl.loop(0, 2 * NJ)
        def _(i):
            n, j = i // NJ, i % NJ
            value = product(0, n, g, j)
            grad[n, pl.ds(mult(g * W), W), pl.ds(mult(j * W), W)] = value
            hi, lo = split(value)
            rows, cols = pl.ds(mult(W + g * W), W), pl.ds(mult(W + j * W), W)
            xs[1, n, 0, rows, cols] = hi
            xs[1, n, 1, rows, cols] = lo
            for m in range(2):

                @pl.when((t == 0) & (i == (m + 1) * NJ - 1))
                def _():
                    row_copy(1, m).start()

        start_cols(1, t)

        @pl.when(t == 3)
        def _():
            b_far(1)
            pass_on(1, relay_turn != 2)
            b_near(1, (0,))
            pass_on(1, relay_turn == 2)
            b_near(1, (1, 2))
            b_pass(1)

    def finish(g, j):
        @pl.loop(0, 2)
        def _(n):
            rows, cols = pl.ds(mult(g * W), W), pl.ds(mult(j * W), W)
            dens[n, rows, cols] = dens[n, rows, cols] + grad[n, rows, cols] + 0.5 * product(1, n, g, j)

    @pl.loop(0, NG)
    def _(t):
        g = order(1, t)
        take_cols(1, 0, g)

        @pl.when(t == 2)
        def _():
            take_rows(1, 0)

        finish(g, 1 - core)

    @pl.loop(0, NG)
    def _(t):
        g = order(1, t)

        @pl.when(has_y)
        def _():
            take_cols(1, 1, g)

        finish(g, core)

    def sent_rows(s):
        for n in range(2):
            row_copy(s, n).wait_send()

        @pl.when(has_b)
        def _():
            for i in range(4):
                b_direct(s, i).wait_send()

        for i in range(1, 4):

            @pl.when(i > depth)
            def _():
                b_second(s, i).wait_send()

    sent_rows(0)
    for s in range(2):

        @pl.loop(0, NG)
        def _(g):
            for n in range(2):
                col_copy(s, 0, n, g).wait_send()

            @pl.when(has_y)
            def _():
                for n in range(2):
                    col_copy(s, 1, n, g).wait_send()

    @pl.when(is_relay)
    def _():
        for s in range(2):
            relay_copy(s).wait_send()

    for q in LATE:

        @pl.when(last & (core == q))
        def _():
            above_copy(q).wait_send()

        @pl.when(first & (core == q))
        def _():
            swap_copy(q).wait_send()

    @pl.when(jnp.logical_not(is_src) & (core == 0))
    def _():
        for p in LATE:
            mate_copy(p).wait_send()

    for q in range(6):

        @pl.when(goes_across(q))
        def _():
            across_copy(q).wait_send()

        @pl.when(goes_back(q))
        def _():
            back_copy(q).wait_send()

        @pl.when(goes_along(q))
        def _():
            along_copy(q).wait_send()

    @pl.when(has_b)
    def _():
        for i in range(4):
            last_part(i)

    sent_rows(1)


def shards(dens_real, dens_imag, upper_band, pattern):
    dma = pltpu.SemaphoreType.DMA
    anywhere = pl.BlockSpec(memory_space=pl.ANY)
    out = pl.pallas_call(
        kernel,
        out_shape=pltpu.VMEM((2, TR, TC), F32),
        in_specs=[anywhere] * 3 + [pl.BlockSpec(memory_space=pltpu.SMEM)],
        out_specs=pl.BlockSpec(memory_space=pltpu.VMEM),
        scratch_shapes=[
            pltpu.VMEM((2, TR, TC), F32),
            pltpu.VMEM((2, 2, 2, TR + 2 * W, TC + 2 * W), BF16),
            pltpu.VMEM((2, 2, 2, W, TC), F32),
            pltpu.VMEM((2, 2, 2, TR, W), F32),
            pltpu.VMEM((TR + W, 3 * BS), F32),
            pltpu.VMEM((TC + W, 3 * BS), F32),
            pltpu.VMEM((2, NG, W, 3 * W), BF16),
            pltpu.VMEM((2, NJ, 3 * W, W), BF16),
            pltpu.VMEM((2, W, W), F32),
            pltpu.VMEM((2, 4, BS, TC), F32),
            dma((9,)),
            dma((2, 2)),
            dma((2, 2)),
            dma((2, 4)),
            dma((2, 4)),
            dma((2, 4)),
            dma((2, 4)),
            dma((2, 2, 2, NG)),
            dma((2, 2, 2, NG)),
            dma((2,)),
            dma((2,)),
            dma((2,)),
            dma((2,)),
            dma((6,)),
            dma((6,)),
            dma((6,)),
            dma((6,)),
            dma((2,)),
            dma((2,)),
        ],
        compiler_params=pltpu.CompilerParams(collective_id=0, has_side_effects=True, vmem_limit_bytes=55 << 20),
        name="heun",
    )(dens_real, dens_imag, upper_band, pattern.T)
    return out[0], out[1]


def solution(mesh):
    in_specs = (P("row", "col"), P("row", "col"), P("row", None), P("row", None))
    out_specs = (P("row", "col"), P("row", "col"))
    return jax.shard_map(shards, mesh=mesh, in_specs=in_specs, out_specs=out_specs, check_vma=False)
```
